256 devices in a mesh: px: 32 (over z_lo, y, x), py: 8 (over z_hi, core).
Axes of the slice: x: 4, y: 4, z: 8 (z_hi: 4, z_lo: 2; z = z_hi * 2 + z_lo), core: 2. Of those that a mesh axis runs over, the one named last changes fastest.
Arguments:
- log_source: float32 [256, 256, 256], P('px', 'py'), may hold values from -12 to 240, as said below
- log_target: float32 [256, 256, 256], P('px', 'py'), may hold values from -12 to 240, as said below
Outputs:
- potential_f: float32 [256, 256, 256], P('px', 'py')
- potential_g: float32 [256, 256, 256], P('px', 'py')
The draws below stay inside these ranges and needn't reach their ends.
Inputs may be any that keep to these rules, and one draw needn't show every extreme that they name: `log_source`: Log-density values on every cell. `log_target`: Log-density values on every cell.
All inputs are finite; a program needn't handle non-finite values.
Results may differ from the reference program's by a relative error of at most 0.0001.
Values sent between devices are 32-bit elements; how exact they have to be, the bound alone decides.
A program may use at most 128 MiB of HBM per device.

```python
import math
import jax
import jax.numpy as jnp
from jax import lax

N = 256
LEVELS = 3
ITERS = 2
FINE_ITERS = 1
BAND = 16


def density_field(key, salt):
    noise_key = jax.random.fold_in(key, salt)
    coords = (jnp.arange(N, dtype=jnp.float32) + 0.5) / N
    first = coords[:, None, None]
    second = coords[None, :, None]
    third = coords[None, None, :]
    smooth = 1.5 * jnp.cos(6.2831853 * first) * jnp.sin(6.2831853 * (second + third))
    rough = jnp.clip(2.0 * jax.random.normal(noise_key, (N, N, N), jnp.float32), -10.0, 10.0)
    return rough + smooth


def draw_log_source(key, part):
    return density_field(key, 11)


def draw_log_target(key, part):
    return density_field(key, 23)


def setup_inputs(seed: int = 0) -> dict:
    key_list = jax.random.split(jax.random.key(seed), 3)
    log_source = draw_log_source(jax.random.fold_in(key_list[2], 71), 0)
    log_target = draw_log_target(jax.random.fold_in(key_list[2], 71), 0)
    return dict(log_source=log_source, log_target=log_target)


def epsilon_of(level_index):
    return 0.05 * 2.0 ** (LEVELS - 1 - level_index)


def soft_axis(values, along, level_index):
    inverse_width = 2.0 ** (LEVELS - 1 - level_index) / 18.0
    window = [1, 1, 1]
    window[along] = 2 * BAND + 1
    padding = [(0, 0), (0, 0), (0, 0)]
    padding[along] = (BAND, BAND)
    line_max = lax.reduce_window(values, -jnp.inf, lax.max, tuple(window), (1, 1, 1), tuple(padding))
    padded = jnp.pad(values, padding, constant_values=-jnp.inf)
    length = values.shape[along]
    summed = jnp.zeros_like(values)
    for offset in range(2 * BAND + 1):
        shifted = lax.slice_in_dim(padded, offset, offset + length, axis=along)
        weight = math.exp(-float((offset - BAND) ** 2) * inverse_width)
        summed = summed + weight * jnp.exp(shifted - line_max)
    return line_max + jnp.log(summed)


def soft_all(values, level_index):
    for along in (2, 1, 0):
        values = soft_axis(values, along, level_index)
    return values


def restrict(values):
    size_a, size_b, size_c = values.shape
    blocks = values.reshape(size_a // 2, 2, size_b // 2, 2, size_c // 2, 2)
    block_max = jnp.max(blocks, axis=(1, 3, 5), keepdims=True)
    merged = block_max + jnp.log(jnp.mean(jnp.exp(blocks - block_max), axis=(1, 3, 5), keepdims=True))
    return merged.reshape(size_a // 2, size_b // 2, size_c // 2)


def prolong(values):
    return jnp.repeat(jnp.repeat(jnp.repeat(values, 2, axis=0), 2, axis=1), 2, axis=2)


def reference(log_source, log_target):
    sources = [log_source]
    targets = [log_target]
    for level_index in range(LEVELS - 1):
        sources = sources + [restrict(sources[-1])]
        targets = targets + [restrict(targets[-1])]
    sources = sources[::-1]
    targets = targets[::-1]
    potential_g = jnp.zeros_like(sources[0])
    potential_f = potential_g
    for level_index in range(LEVELS):
        epsilon = epsilon_of(level_index)
        sweeps = FINE_ITERS if level_index == LEVELS - 1 else ITERS
        for iteration in range(sweeps):
            potential_f = epsilon * (sources[level_index] - soft_all(potential_g / epsilon, level_index))
            potential_g = epsilon * (targets[level_index] - soft_all(potential_f / epsilon, level_index))
        if level_index < LEVELS - 1:
            potential_g = prolong(potential_g)
    return potential_f, potential_g
```

```python
import math

import jax
import jax.numpy as jnp
from jax import lax
from jax.experimental import pallas as pl
from jax.experimental.pallas import tpu as pltpu
from jax.sharding import PartitionSpec as P

LEVELS = 3
BAND = 16
NEG = -1e30
LOG2E = 1.4426950408889634
LN2 = 0.6931471805599453
MESH = pl.DeviceIdType.MESH
HIGHEST = lax.Precision.HIGHEST


def taps_of(level):
    inverse_width = 2.0 ** (LEVELS - 1 - level) / 18.0
    return [math.exp(-float(d * d) * inverse_width) for d in range(BAND + 1)]


def coarse_taps(level):
    taps = taps_of(level)
    weights = []
    for s in range(2):
        weights.append(
            [
                sum(taps[abs(2 * D + u - s)] for u in range(2) if abs(2 * D + u - s) <= BAND)
                for D in range(-BAND // 2, BAND // 2 + 1)
            ]
        )
    return weights


def lane_lo(shape):
    return lax.broadcasted_iota(jnp.int32, shape, 1) < 64


def half(v):
    return pltpu.roll(v, 64, 1)


def mix(a, b):
    lo = lane_lo(a.shape)
    return jnp.where(lo, a, half(b)), jnp.where(lo, half(a), b)


def tree(op, xs):
    xs = list(xs)
    while len(xs) > 1:
        xs = [op(xs[i], xs[i + 1]) if i + 1 < len(xs) else xs[i] for i in range(0, len(xs), 2)]
    return xs[0]


def soft_rows(pad, planes, n, level, store, chunk=16):
    taps = taps_of(level)
    per = n // chunk

    def body(it, carry):
        p = it // per
        c = pl.multiple_of((it % per) * chunk, chunk)

        def tap(d):
            return pad[p, pl.ds(c + d, chunk), :]

        m = tree(jnp.maximum, [tap(d) for d in range(2 * BAND + 1)])
        parts = [jnp.exp2(tap(BAND) - m)]
        for d in range(1, BAND + 1):
            pair = jnp.exp2(tap(BAND - d) - m) + jnp.exp2(tap(BAND + d) - m)
            parts.append(taps[d] * pair)
        accs = [tree(jnp.add, parts[i::4]) for i in range(4)]
        total = (accs[0] + accs[1]) + (accs[2] + accs[3])
        store(p, c, m + jnp.log2(total))
        return carry

    lax.fori_loop(0, planes * per, body, 0)


def soft_rows_copied(pad, planes, first, n, level, store, chunk=16):
    weights = coarse_taps(level)
    per = n // chunk

    def body(it, carry):
        p = it // per
        c = pl.multiple_of((it % per) * chunk, chunk)

        def tap(t):
            return pad[p, pl.ds(first + c + BAND // 2 + t, chunk), :]

        m = tree(jnp.maximum, [tap(t) for t in range(BAND + 1)])
        es = [jnp.exp2(tap(t) - m) for t in range(BAND + 1)]
        for s in range(2):
            total = tree(jnp.add, [weights[s][t] * es[t] for t in range(BAND + 1)])
            store(p, c, s, m + jnp.log2(total))
        return carry

    lax.fori_loop(0, planes * per, body, 0)


def border(pad, n):
    planes, _, lanes = pad.shape
    for p in range(planes):
        pad[p, pl.ds(0, BAND), :] = jnp.full((BAND, lanes), NEG, jnp.float32)
        pad[p, pl.ds(BAND + n, BAND), :] = jnp.full((BAND, lanes), NEG, jnp.float32)


def pair_max(v, axis):
    n = v.shape[axis]
    even = lax.broadcasted_iota(jnp.int32, v.shape, axis) % 2 == 0
    other = jnp.where(even, pltpu.roll(v, n - 1, axis), pltpu.roll(v, 1, axis))
    return jnp.maximum(v, other)


def halving(rows, cols, axis, shift=0):
    i = lax.broadcasted_iota(jnp.int32, (rows, cols), 0)
    j = lax.broadcasted_iota(jnp.int32, (rows, cols), 1)
    if axis == 0:
        return (j // 2 == i).astype(jnp.float32)
    return (i // 2 + shift == j).astype(jnp.float32)


def mm(a, b):
    return jnp.dot(a, b, precision=HIGHEST, preferred_element_type=jnp.float32)


def weight_log(pos, level, n):
    taps = taps_of(level)
    total = jnp.zeros(pos.shape, jnp.float32)
    for d in range(-BAND, BAND + 1):
        inside = (pos + d >= 0) & (pos + d < n)
        total = total + jnp.where(inside, taps[abs(d)], 0.0)
    return jnp.log2(total)


ROUNDS = [
    "g0", "g1", "s2a", "s2b", "x0", "l0a", "l0b", "l0c", "x1", "l1p", "l1a", "l1b", "l1c",
    "l2p", "l2a", "l2b", "fa", "fb",
]


def kernel(src, tgt, f_out, g_out, *scratch):
    names = [name for name, _ in SCRATCH]
    ref = dict(zip(names, scratch))
    send_sem, recv_sem = scratch[-2], scratch[-1]
    px = lax.axis_index("px")
    py = lax.axis_index("py")
    zh = py // 2
    core = py % 2
    g = 2 * px + core

    barrier = pltpu.get_barrier_semaphore()

    def in_group(q):
        return (q // 2, 2 * zh + q % 2)

    def greet_group(o, carry):
        pl.semaphore_signal(barrier, inc=1, device_id=in_group((g + o) % 64), device_id_type=MESH)
        return carry

    def greet_column(o, carry):
        peer = (2 * ((zh + o // 2) % 4)) + o % 2
        pl.semaphore_signal(barrier, inc=1, device_id=(px, peer), device_id_type=MESH)
        return carry

    lax.fori_loop(1, 64, greet_group, 0)
    lax.fori_loop(2, 8, greet_column, 0)

    def exchange(name, n, me, device, src_at, dst_at):
        k = ROUNDS.index(name)

        def one(o, carry):
            q = (me + o) % n
            pltpu.make_async_remote_copy(
                src_ref=src_at(q),
                dst_ref=dst_at(me),
                send_sem=send_sem.at[k],
                recv_sem=recv_sem.at[k],
                device_id=device(q),
                device_id_type=MESH,
            ).start()
            return carry

        lax.fori_loop(1, n, one, 0)
        pltpu.make_async_copy(src_at(me), dst_at(me), recv_sem.at[k]).start()

    def arrived(name, whole):
        k = ROUNDS.index(name)
        pltpu.make_async_copy(whole, whole, recv_sem.at[k]).wait()

    def sent(name, part):
        k = ROUNDS.index(name)
        pltpu.make_async_copy(part, part, send_sem.at[k]).wait()

    def column(q):
        return (px, q)

    def pencil(q):
        return (q, py)

    def depth(q):
        return (px, 2 * q + core)

    es, ms = [], []
    for arr in (src, tgt):
        for d in range(4):
            a = arr[2 * d] * LOG2E
            b = arr[2 * d + 1] * LOG2E
            m = pair_max(pair_max(jnp.maximum(a, b), 0), 1)
            es.append(jnp.exp2(a - m) + jnp.exp2(b - m))
            ms.append(m)
    fine = mm(jnp.concatenate(es + ms, axis=0), halving(256, 128, 1))
    rows = halving(128, 256, 0)
    r1 = mm(rows, fine[256:]) * 0.25 + jnp.log2(mm(rows, fine[:256])) - 3.0
    s1 = ref["g1s"]
    for i in range(8):
        s1[i // 4, i % 4] = r1[16 * i : 16 * i + 16]
    es, ms = [], []
    for d in range(2):
        for arr in range(2):
            o = (arr * 4 + 2 * d) * 16
            a, b = r1[o : o + 16], r1[o + 16 : o + 32]
            m = pair_max(pair_max(jnp.maximum(a, b), 0), 1)
            es.append(jnp.exp2(a - m) + jnp.exp2(b - m))
            ms.append(m)

    def packed(v):
        low = mm(jnp.concatenate(v[:2], axis=0), halving(128, 128, 1))
        high = mm(jnp.concatenate(v[2:], axis=0), halving(128, 128, 1, 64))
        return mm(halving(16, 32, 0), low + high)

    r0 = packed(ms) * 0.25 + jnp.log2(packed(es)) - 3.0
    s0 = ref["g0s"]
    s0[0] = r0[:8]
    s0[1] = r0[8:]

    pl.semaphore_wait(barrier, 69)

    r_g0, r_g1, r_s2a = ref["g0r"], ref["g1r"], ref["s2ar"]
    exchange("g0", 8, py, column, lambda q: s0, lambda q: r_g0.at[q])
    exchange("g1", 8, py, column, lambda q: s1.at[:, pl.ds(2 * (q % 2), 2)], lambda q: r_g1.at[q])
    exchange("s2a", 32, px, pencil, lambda q: src.at[:, q], lambda q: r_s2a.at[pl.ds(8 * q, 8)])

    for name, n in (("m0", 64), ("t0", 64), ("r0", 64), ("m1", 128), ("t1", 128), ("r1", 128), ("c1", 64), ("u2", 128),
                    ("c2", 128), ("m2", 256), ("r2", 256), ("k2", 256)):
        border(ref[name], n)

    m0, t0, q0, w0 = ref["m0"], ref["t0"], ref["r0"], ref["w0"]

    lanes0 = lax.broadcasted_iota(jnp.int32, (64, 128), 1)
    zero0 = (
        weight_log(lax.broadcasted_iota(jnp.int32, (64, 128), 0), 0, 64)
        + weight_log(lanes0 % 64, 0, 64)
        + weight_log(2 * px + lanes0 // 64, 0, 64)
    )

    def turn0(v):
        t = jnp.concatenate([v, v], axis=0).T
        return jnp.where(lane_lo((64, 128)), t[:64], t[64:])

    def scatter0(r, store):
        a, b = mix(r[pl.ds(0, 32, stride=2), :], r[pl.ds(1, 32, stride=2), :])
        store(0, a)
        store(1, b)

    arrived("g0", r_g0)
    x0s, x0r, a0, b0 = ref["x0s"], ref["x0r"], ref["a0"], ref["b0"]
    for i in range(8):
        x0s[8 * i : 8 * i + 8, :] = r_g0[i, 0]
        b0[8 * i : 8 * i + 8, :] = r_g0[i, 1]

    def swap0(name, s, r):
        exchange(name, 32, px, pencil, lambda q: s.at[pl.ds(2 * q, 2)], lambda q: r.at[pl.ds(2 * q, 2)])

    swap0("x0", x0s, x0r)
    arrived("x0", x0r)

    def put_a0(k, v):
        a0[pl.ds(k, 32, stride=2), :] = v

    scatter0(x0r, put_a0)
    m0[0, pl.ds(BAND, 64), :] = a0[...] - zero0

    def transform0(name, other, background):
        s, r = ref[name + "s"], ref[name + "r"]

        def put_w(p, c, v):
            w0[pl.ds(c, 16), :] = v

        soft_rows(m0, 1, 64, 0, put_w)
        t0[0, pl.ds(BAND, 64), :] = turn0(w0[...])
        soft_rows(t0, 1, 64, 0, put_w)
        s[...] = turn0(w0[...])
        swap0(name, s, r)
        background()
        arrived(name, r)

        def put_r(k, v):
            q0[0, pl.ds(BAND + k, 32, stride=2), :] = v

        scatter0(r, put_r)

        def finish(p, c, v):
            m0[0, pl.ds(BAND + c, 16), :] = other[pl.ds(c, 16), :] - v

        soft_rows(q0, 1, 64, 0, finish)

    m1, t1, q1, w1 = ref["m1"], ref["t1"], ref["r1"], ref["w1"]
    a1, b1 = ref["a1"], ref["b1"]

    def swap1(name, s, r):
        exchange(name, 64, g, in_group, lambda q: s.at[pl.ds(4 * q, 4)], lambda q: r.at[pl.ds(4 * q, 4)])

    def gather1(plane_rows, s):
        for a in range(2):
            for b in range(2):
                s[pl.ds(2 * b + a, 64, stride=4), :] = plane_rows(a, b)

    def scatter1(r, store):
        for a in range(2):
            for b in range(2):
                store(b, a, r[pl.ds(2 * b + a, 64, stride=4), :])

    def source1_out():
        arrived("g1", r_g1)
        for i in range(8):
            for a in range(2):
                w1[a, 16 * i : 16 * i + 16, :] = r_g1[i, 0, a]
                b1[a, 16 * i : 16 * i + 16, :] = r_g1[i, 1, a]
        gather1(lambda a, b: w1[a, pl.ds(b, 64, stride=2), :], ref["x1s"])
        swap1("x1", ref["x1s"], ref["x1r"])

    def source2_out():
        arrived("s2a", r_s2a)
        out = ref["s2bs"]
        for pair in range(2):
            cols = slice(128 * pair, 128 * pair + 128)
            a, b = mix(r_s2a[0:128, cols], r_s2a[128:256, cols])
            out[2 * pair] = a
            out[2 * pair + 1] = b
        exchange("s2b", 4, zh, depth, lambda q: out.at[q], lambda q: ref["s2br"].at[q])

    def source1_in():
        arrived("x1", ref["x1r"])

        def put(b, a, v):
            a1[b, pl.ds(a, 64, stride=2), :] = v

        scatter1(ref["x1r"], put)

    transform0("l0a", b0, source1_out)
    transform0("l0b", a0, source2_out)
    transform0("l0c", b0, source1_in)

    g0 = m0[0, pl.ds(BAND, 64), :] * 2.0
    own = jnp.where(core == 0, g0, half(g0))
    c1, u1 = ref["c1"], ref["u1"]
    c1[0, pl.ds(BAND, 64), :] = own

    def put_u(p, c, s, v):
        u1[pl.ds(2 * c + s, 16, stride=2), :] = v

    soft_rows_copied(c1, 1, 0, 64, 1, put_u)
    c1[0, pl.ds(BAND, 64), :] = u1[...].T[:64]
    soft_rows_copied(c1, 1, 0, 64, 1, put_u)
    l1ps, l1pr = ref["l1ps"], ref["l1pr"]
    l1ps[...] = u1[...].T
    exchange("l1p", 64, g, in_group, lambda q: l1ps.at[pl.ds(2 * q, 2)], lambda q: l1pr.at[pl.ds(2 * q, 2)])
    arrived("l1p", l1pr)

    def finish_l1p(b):
        def put(p, c, s, v):
            m1[b, pl.ds(BAND + 2 * c + s, 16, stride=2), :] = a1[b, pl.ds(2 * c + s, 16, stride=2), :] - v

        return put

    for b in range(2):
        c1[0, pl.ds(BAND, 64), :] = l1pr[pl.ds(b, 64, stride=2), :]
        soft_rows_copied(c1, 1, 0, 64, 1, finish_l1p(b))

    def transform1(name, other, background):
        s, r = ref[name + "s"], ref[name + "r"]

        def put_w(p, c, v):
            w1[p, pl.ds(c, 16), :] = v

        soft_rows(m1, 2, 128, 1, put_w)
        for p in range(2):
            t1[p, pl.ds(BAND, 128), :] = w1[p].T
        soft_rows(t1, 2, 128, 1, put_w)
        for p in range(2):
            w1[p] = w1[p].T
        gather1(lambda a, b: w1[a, pl.ds(b, 64, stride=2), :], s)
        swap1(name, s, r)
        background()
        arrived(name, r)

        def put_r(b, a, v):
            q1[b, pl.ds(BAND + a, 64, stride=2), :] = v

        scatter1(r, put_r)

        def finish(p, c, v):
            m1[p, pl.ds(BAND + c, 16), :] = other[p, pl.ds(c, 16), :] - v

        soft_rows(q1, 2, 128, 1, finish)

    a2 = ref["a2"]

    def source2_in():
        arrived("s2b", ref["s2br"])
        r = ref["s2br"]
        for zp in range(2):
            a, b = mix(r[2 * zp], r[2 * zp + 1])
            a2[zp, 0:128, :] = a * LOG2E
            a2[zp, 128:256, :] = b * LOG2E

    transform1("l1a", b1, source2_in)
    transform1("l1b", a1, lambda: None)
    transform1("l1c", b1, lambda: None)

    u2, w2, l2ps, l2pr = ref["u2"], ref["w2"], ref["l2ps"], ref["l2pr"]
    for a in range(2):
        t1[a, pl.ds(BAND, 128), :] = m1[a, pl.ds(BAND, 128), :].T * 2.0

    def put_w2(p, c, s, v):
        w2[pl.ds(64 * p + 2 * c + s, 16, stride=2), :] = v

    soft_rows_copied(t1, 2, pl.multiple_of(32 * zh, 32), 32, 2, put_w2)
    u2[0, pl.ds(BAND, 128), :] = w2[...].T

    def put_l2p(p, c, s, v):
        l2ps[c // 32, pl.ds(2 * (c % 32) + s, 16, stride=2), :] = v

    soft_rows_copied(u2, 1, 0, 128, 2, put_l2p)
    exchange(
        "l2p", 64, g, in_group,
        lambda q: l2ps.at[:, pl.ds(32 * (q % 2) + q // 2, 1)],
        lambda q: l2pr.at[:, pl.ds(q, 1)],
    )
    arrived("l2p", l2pr)
    c2, m2 = ref["c2"], ref["m2"]
    for zp in range(2):
        a, b = mix(l2pr[2 * zp], l2pr[2 * zp + 1])
        c2[zp, pl.ds(BAND, 64, stride=2), :] = a
        c2[zp, pl.ds(BAND + 1, 64, stride=2), :] = b

    def put_m2(p, c, s, v):
        m2[p, pl.ds(BAND + 2 * c + s, 16, stride=2), :] = a2[p, pl.ds(2 * c + s, 16, stride=2), :] - v

    soft_rows_copied(c2, 2, 0, 128, 2, put_m2)

    scale = 0.05 * LN2
    fas, far = ref["fas"], ref["far"]
    for zp in range(2):
        a, b = mix(m2[zp, pl.ds(BAND, 128), :], m2[zp, pl.ds(BAND + 128, 128), :])
        fas[2 * zp] = a * scale
        fas[2 * zp + 1] = b * scale
    exchange("fa", 4, zh, depth, lambda q: fas.at[q], lambda q: far.at[q])

    l2as, l2ar = ref["l2as"], ref["l2ar"]

    def put_l2a(p, c, v):
        l2as[p, pl.ds(c, 16), :] = v

    soft_rows(m2, 2, 256, 2, put_l2a)
    slot = 32 * core + px
    k2a = ROUNDS.index("l2a")

    def send_l2a(o, carry):
        q = (g + o) % 64
        pltpu.make_async_remote_copy(
            src_ref=l2as.at[:, pl.ds(4 * q, 4)],
            dst_ref=l2ar.at[:, pl.ds(4 * slot, 4)],
            send_sem=send_sem.at[k2a],
            recv_sem=recv_sem.at[k2a],
            device_id=in_group(q),
            device_id_type=MESH,
        ).start()
        return carry

    lax.fori_loop(1, 64, send_l2a, 0)
    pltpu.make_async_copy(l2as.at[:, pl.ds(4 * g, 4)], l2ar.at[:, pl.ds(4 * slot, 4)], recv_sem.at[k2a]).start()

    arrived("fa", far)
    fbs, fbr = ref["fbs"], ref["fbr"]
    for pair in range(2):
        a, b = mix(far[2 * pair], far[2 * pair + 1])
        fbs[pair, 0:128, :] = a
        fbs[pair, 128:256, :] = b
    arrived("l2a", l2ar)
    exchange("fb", 32, px, pencil, lambda q: fbs.at[:, pl.ds(8 * q, 8)], lambda q: fbr.at[:, pl.ds(8 * q, 8)])

    q2, l2bs, l2br = ref["r2"], ref["l2bs"], ref["l2br"]
    for zp in range(2):
        for tp in range(2):
            a, b = mix(
                l2ar[zp, pl.ds(2 * tp, 64, stride=4), :], l2ar[zp, pl.ds(2 * tp + 1, 64, stride=4), :]
            )
            q2[tp, pl.ds(BAND + 128 * zp, 64), :] = a
            q2[tp, pl.ds(BAND + 128 * zp + 64, 64), :] = b

    def put_l2b(p, c, v):
        l2bs[p, pl.ds(c, 16), :] = v

    soft_rows(q2, 2, 256, 2, put_l2b)
    exchange("l2b", 8, py, column, lambda q: l2bs.at[:, pl.ds(32 * q, 32)], lambda q: l2br.at[q])
    arrived("fb", fbr)
    for d in range(8):
        for h in range(2):
            f_out[d, :, 128 * h : 128 * h + 128] = fbr[h, pl.ds(d, 32, stride=8), :]
    arrived("l2b", l2br)
    k2, w3 = ref["k2"], ref["w3"]
    for z in range(4):
        t = l2br[2 * z : 2 * z + 2].reshape(128, 128).T
        for tt in range(2):
            k2[tt, pl.ds(BAND + 64 * z, 64), :] = t[64 * tt : 64 * tt + 64]

    def put_w3(p, c, v):
        w3[p, pl.ds(c, 16), :] = v

    soft_rows(k2, 2, 256, 2, put_w3)
    for tt in range(2):
        for h in range(2):
            t = w3[tt, 128 * h : 128 * h + 128, :].T
            for c in range(4):
                cols = slice(128 * h, 128 * h + 128)
                g_out[2 * c + tt, :, cols] = tgt[2 * c + tt, :, cols] * 0.05 - t[32 * c : 32 * c + 32] * scale

    sent("g0", r_g0.at[pl.ds(0, 7)])
    sent("g1", r_g1.at[pl.ds(0, 7)])
    sent("s2a", r_s2a.at[pl.ds(0, 248)])
    sent("s2b", ref["s2br"].at[pl.ds(0, 3)])
    for name in ("x0", "l0a", "l0b", "l0c"):
        sent(name, ref[name + "r"].at[pl.ds(0, 62)])
    for name in ("x1", "l1a", "l1b", "l1c"):
        sent(name, ref[name + "r"].at[pl.ds(0, 252)])
    sent("l1p", l1pr.at[pl.ds(0, 126)])
    sent("l2p", l2pr.at[:, pl.ds(0, 63)])
    sent("l2a", l2ar.at[:, pl.ds(0, 252)])
    sent("l2b", l2br.at[pl.ds(0, 7)])
    sent("fa", far.at[pl.ds(0, 3)])
    sent("fb", fbr.at[:, pl.ds(0, 248)])


SCRATCH = [
    ("g0s", (2, 8, 128)), ("g0r", (8, 2, 8, 128)),
    ("g1s", (2, 4, 16, 128)), ("g1r", (8, 2, 2, 16, 128)),
    ("s2ar", (256, 256)), ("s2bs", (4, 128, 128)), ("s2br", (4, 128, 128)),
    ("x0s", (64, 128)), ("x0r", (64, 128)),
    ("l0as", (64, 128)), ("l0ar", (64, 128)), ("l0bs", (64, 128)), ("l0br", (64, 128)),
    ("l0cs", (64, 128)), ("l0cr", (64, 128)),
    ("x1s", (256, 128)), ("x1r", (256, 128)),
    ("l1ps", (128, 128)), ("l1pr", (128, 128)),
    ("l1as", (256, 128)), ("l1ar", (256, 128)), ("l1bs", (256, 128)), ("l1br", (256, 128)),
    ("l1cs", (256, 128)), ("l1cr", (256, 128)),
    ("l2ps", (4, 64, 128)), ("l2pr", (4, 64, 128)),
    ("l2as", (2, 256, 128)), ("l2ar", (2, 256, 128)),
    ("l2bs", (2, 256, 128)), ("l2br", (8, 2, 32, 128)),
    ("fas", (4, 128, 128)), ("far", (4, 128, 128)), ("fbs", (2, 256, 128)), ("fbr", (2, 256, 128)),
    ("m0", (1, 96, 128)), ("t0", (1, 96, 128)), ("r0", (1, 96, 128)), ("w0", (64, 128)),
    ("a0", (64, 128)), ("b0", (64, 128)),
    ("m1", (2, 160, 128)), ("t1", (2, 160, 128)), ("r1", (2, 160, 128)), ("w1", (2, 128, 128)),
    ("a1", (2, 128, 128)), ("b1", (2, 128, 128)),
    ("c1", (1, 96, 128)), ("u1", (128, 128)),
    ("u2", (1, 160, 128)), ("w2", (128, 128)), ("c2", (2, 160, 128)), ("a2", (2, 256, 128)),
    ("m2", (2, 288, 128)), ("r2", (2, 288, 128)), ("k2", (2, 288, 128)), ("w3", (2, 256, 128)),
]


def per_device(log_source, log_target):
    shape = jax.ShapeDtypeStruct((8, 32, 256), jnp.float32)
    vmem = pl.BlockSpec(memory_space=pltpu.VMEM)
    return pl.pallas_call(
        kernel,
        out_shape=(shape, shape),
        in_specs=[vmem, vmem],
        out_specs=(vmem, vmem),
        scratch_shapes=[pltpu.VMEM(s, jnp.float32) for _, s in SCRATCH]
        + [pltpu.SemaphoreType.DMA((len(ROUNDS),)), pltpu.SemaphoreType.DMA((len(ROUNDS),))],
        compiler_params=pltpu.CompilerParams(collective_id=0, has_side_effects=True),
        name="sinkhorn",
    )(log_source, log_target)


def solution(mesh):
    return jax.shard_map(
        per_device,
        mesh=mesh,
        in_specs=(P("px", "py", None), P("px", "py", None)),
        out_specs=(P("px", "py", None), P("px", "py", None)),
        check_vma=False,
    )
```

```python
import math

import jax
import jax.numpy as jnp
from jax import lax
from jax.experimental import pallas as pl
from jax.experimental.pallas import tpu as pltpu
from jax.sharding import PartitionSpec as P

LEVELS = 3
BAND = 16
NEG = -1e30
LOG2E = 1.4426950408889634
LN2 = 0.6931471805599453
MESH = pl.DeviceIdType.MESH
HIGHEST = lax.Precision.HIGHEST


def taps_of(level):
    inverse_width = 2.0 ** (LEVELS - 1 - level) / 18.0
    return [math.exp(-float(d * d) * inverse_width) for d in range(BAND + 1)]


def coarse_taps(level):
    taps = taps_of(level)
    weights = []
    for s in range(2):
        weights.append(
            [
                sum(taps[abs(2 * D + u - s)] for u in range(2) if abs(2 * D + u - s) <= BAND)
                for D in range(-BAND // 2, BAND // 2 + 1)
            ]
        )
    return weights


def lane_lo(shape):
    return lax.broadcasted_iota(jnp.int32, shape, 1) < 64


def half(v):
    return pltpu.roll(v, 64, 1)


def mix(a, b):
    lo = lane_lo(a.shape)
    return jnp.where(lo, a, half(b)), jnp.where(lo, half(a), b)


def tree(op, xs):
    xs = list(xs)
    while len(xs) > 1:
        xs = [op(xs[i], xs[i + 1]) if i + 1 < len(xs) else xs[i] for i in range(0, len(xs), 2)]
    return xs[0]


def soft_rows(pad, planes, n, level, store, chunk=16):
    taps = taps_of(level)
    per = n // chunk

    def body(it, carry):
        p = it // per
        c = pl.multiple_of((it % per) * chunk, chunk)

        def tap(d):
            return pad[p, pl.ds(c + d, chunk), :]

        m = tree(jnp.maximum, [tap(d) for d in range(2 * BAND + 1)])
        parts = [jnp.exp2(tap(BAND) - m)]
        for d in range(1, BAND + 1):
            pair = jnp.exp2(tap(BAND - d) - m) + jnp.exp2(tap(BAND + d) - m)
            parts.append(taps[d] * pair)
        accs = [tree(jnp.add, parts[i::4]) for i in range(4)]
        total = (accs[0] + accs[1]) + (accs[2] + accs[3])
        store(p, c, m + jnp.log2(total))
        return carry

    lax.fori_loop(0, planes * per, body, 0)


def soft_rows_copied(pad, planes, first, n, level, store, chunk=16):
    weights = coarse_taps(level)
    per = n // chunk

    def body(it, carry):
        p = it // per
        c = pl.multiple_of((it % per) * chunk, chunk)

        def tap(t):
            return pad[p, pl.ds(first + c + BAND // 2 + t, chunk), :]

        m = tree(jnp.maximum, [tap(t) for t in range(BAND + 1)])
        es = [jnp.exp2(tap(t) - m) for t in range(BAND + 1)]
        for s in range(2):
            total = tree(jnp.add, [weights[s][t] * es[t] for t in range(BAND + 1)])
            store(p, c, s, m + jnp.log2(total))
        return carry

    lax.fori_loop(0, planes * per, body, 0)


def soft_major(buf, n, level, store, rows=2):
    taps = taps_of(level)
    per = n // rows

    def body(it, carry):
        h = it // per
        c = (it % per) * rows
        for r in range(rows):

            def tap(d):
                return buf[c + r + d, h]

            m = tree(jnp.maximum, [tap(d) for d in range(2 * BAND + 1)])
            parts = [jnp.exp2(tap(BAND) - m)]
            for d in range(1, BAND + 1):
                pair = jnp.exp2(tap(BAND - d) - m) + jnp.exp2(tap(BAND + d) - m)
                parts.append(taps[d] * pair)
            accs = [tree(jnp.add, parts[i::4]) for i in range(4)]
            total = (accs[0] + accs[1]) + (accs[2] + accs[3])
            store(c + r, h, m + jnp.log2(total))
        return carry

    lax.fori_loop(0, 2 * per, body, 0)


def border(pad, n):
    planes, _, lanes = pad.shape
    for p in range(planes):
        pad[p, pl.ds(0, BAND), :] = jnp.full((BAND, lanes), NEG, jnp.float32)
        pad[p, pl.ds(BAND + n, BAND), :] = jnp.full((BAND, lanes), NEG, jnp.float32)


def pair_max(v, axis):
    n = v.shape[axis]
    even = lax.broadcasted_iota(jnp.int32, v.shape, axis) % 2 == 0
    other = jnp.where(even, pltpu.roll(v, n - 1, axis), pltpu.roll(v, 1, axis))
    return jnp.maximum(v, other)


def halving(rows, cols, axis, shift=0):
    i = lax.broadcasted_iota(jnp.int32, (rows, cols), 0)
    j = lax.broadcasted_iota(jnp.int32, (rows, cols), 1)
    if axis == 0:
        return (j // 2 == i).astype(jnp.float32)
    return (i // 2 + shift == j).astype(jnp.float32)


def mm(a, b):
    return jnp.dot(a, b, precision=HIGHEST, preferred_element_type=jnp.float32)


def weight_log(pos, level, n):
    taps = taps_of(level)
    total = jnp.zeros(pos.shape, jnp.float32)
    for d in range(-BAND, BAND + 1):
        inside = (pos + d >= 0) & (pos + d < n)
        total = total + jnp.where(inside, taps[abs(d)], 0.0)
    return jnp.log2(total)


ROUNDS = [
    "g0", "g1", "s2a", "x0", "l0a", "l0b", "l0c", "x1", "l1p", "l1a", "l1b", "l1c",
    "l2p", "l2own", "l2up", "l2down", "fb",
]


def kernel(src, tgt, f_out, g_out, *scratch):
    names = [name for name, _ in SCRATCH]
    ref = dict(zip(names, scratch))
    send_sem, recv_sem = scratch[-2], scratch[-1]
    px = lax.axis_index("px")
    py = lax.axis_index("py")
    zh = py // 2
    core = py % 2
    g = 2 * px + core

    barrier = pltpu.get_barrier_semaphore()

    def in_group(q):
        return (q // 2, 2 * zh + q % 2)

    def greet_group(o, carry):
        pl.semaphore_signal(barrier, inc=1, device_id=in_group((g + o) % 64), device_id_type=MESH)
        return carry

    def greet_column(o, carry):
        peer = (2 * ((zh + o // 2) % 4)) + o % 2
        pl.semaphore_signal(barrier, inc=1, device_id=(px, peer), device_id_type=MESH)
        return carry

    lax.fori_loop(1, 64, greet_group, 0)
    lax.fori_loop(2, 8, greet_column, 0)

    side = jnp.where(core == 0, py - 1, py + 1)
    has_side = (side >= 0) & (side < 8)

    @pl.when(has_side)
    def _():
        def greet_side(o, carry):
            pl.semaphore_signal(barrier, inc=1, device_id=((px + o) % 32, side), device_id_type=MESH)
            return carry

        lax.fori_loop(1, 32, greet_side, 0)

    leaving = []

    def exchange(name, n, me, device, src_at, dst_at, most):
        k = ROUNDS.index(name)

        def one(o, carry):
            q = (me + o) % n
            pltpu.make_async_remote_copy(
                src_ref=src_at(q),
                dst_ref=dst_at(me),
                send_sem=send_sem.at[k],
                recv_sem=recv_sem.at[k],
                device_id=device(q),
                device_id_type=MESH,
            ).start()
            return carry

        lax.fori_loop(1, n, one, 0)
        pltpu.make_async_copy(src_at(me), dst_at(me), recv_sem.at[k]).start()
        leaving.append((name, most))

    def arrived(name, whole):
        k = ROUNDS.index(name)
        pltpu.make_async_copy(whole, whole, recv_sem.at[k]).wait()

    def sent(name, part):
        k = ROUNDS.index(name)
        pltpu.make_async_copy(part, part, send_sem.at[k]).wait()

    def column(q):
        return (px, q)

    def pencil(q):
        return (q, py)

    def depth(q):
        return (px, 2 * q + core)

    es, ms = [], []
    for arr in (src, tgt):
        for d in range(4):
            a = arr[2 * d] * LOG2E
            b = arr[2 * d + 1] * LOG2E
            m = pair_max(pair_max(jnp.maximum(a, b), 0), 1)
            es.append(jnp.exp2(a - m) + jnp.exp2(b - m))
            ms.append(m)
    fine = mm(jnp.concatenate(es + ms, axis=0), halving(256, 128, 1))
    rows = halving(128, 256, 0)
    r1 = mm(rows, fine[256:]) * 0.25 + jnp.log2(mm(rows, fine[:256])) - 3.0
    s1 = ref["g1s"]
    for i in range(8):
        s1[i // 4, i % 4] = r1[16 * i : 16 * i + 16]
    es, ms = [], []
    for d in range(2):
        for arr in range(2):
            o = (arr * 4 + 2 * d) * 16
            a, b = r1[o : o + 16], r1[o + 16 : o + 32]
            m = pair_max(pair_max(jnp.maximum(a, b), 0), 1)
            es.append(jnp.exp2(a - m) + jnp.exp2(b - m))
            ms.append(m)

    def packed(v):
        low = mm(jnp.concatenate(v[:2], axis=0), halving(128, 128, 1))
        high = mm(jnp.concatenate(v[2:], axis=0), halving(128, 128, 1, 64))
        return mm(halving(16, 32, 0), low + high)

    r0 = packed(ms) * 0.25 + jnp.log2(packed(es)) - 3.0
    s0 = ref["g0s"]
    s0[0] = r0[:8]
    s0[1] = r0[8:]

    pl.semaphore_wait(barrier, jnp.where(has_side, 100, 69))

    r_g0, r_g1, r_s2a = ref["g0r"], ref["g1r"], ref["s2ar"]
    exchange("g0", 8, py, column, lambda q: s0, lambda q: r_g0.at[q], r_g0.at[pl.ds(0, 7)])

    for name, n in (("m0", 64), ("t0", 64), ("r0", 64), ("m1", 128), ("t1", 128), ("r1", 128), ("c1", 64), ("u2", 128),
                    ("l2pr", 128), ("m2", 256), ("k2", 256)):
        border(ref[name], n)

    m0, t0, q0, w0 = ref["m0"], ref["t0"], ref["r0"], ref["w0"]

    lanes0 = lax.broadcasted_iota(jnp.int32, (64, 128), 1)
    zero0 = (
        weight_log(lax.broadcasted_iota(jnp.int32, (64, 128), 0), 0, 64)
        + weight_log(lanes0 % 64, 0, 64)
        + weight_log(2 * px + lanes0 // 64, 0, 64)
    )

    def turn0(v):
        t = jnp.concatenate([v, v], axis=0).T
        return jnp.where(lane_lo((64, 128)), t[:64], t[64:])

    def scatter0(r, store):
        a, b = mix(r[pl.ds(0, 32, stride=2), :], r[pl.ds(1, 32, stride=2), :])
        store(0, a)
        store(1, b)

    arrived("g0", r_g0)
    x0s, x0r, a0, b0 = ref["x0s"], ref["x0r"], ref["a0"], ref["b0"]
    for i in range(8):
        x0s[8 * i : 8 * i + 8, :] = r_g0[i, 0]
        b0[8 * i : 8 * i + 8, :] = r_g0[i, 1]

    def swap0(name, s, r):
        exchange(name, 32, px, pencil, lambda q: s.at[pl.ds(2 * q, 2)], lambda q: r.at[pl.ds(2 * q, 2)], r.at[pl.ds(0, 62)])

    swap0("x0", x0s, x0r)
    exchange("g1", 8, py, column, lambda q: s1.at[:, pl.ds(2 * (q % 2), 2)], lambda q: r_g1.at[q], r_g1.at[pl.ds(0, 7)])
    arrived("x0", x0r)

    def put_a0(k, v):
        a0[pl.ds(k, 32, stride=2), :] = v

    scatter0(x0r, put_a0)
    m0[0, pl.ds(BAND, 64), :] = a0[...] - zero0

    def transform0(name, other, background):
        s, r = ref[name + "s"], ref[name + "r"]

        def put_w(p, c, v):
            w0[pl.ds(c, 16), :] = v

        soft_rows(m0, 1, 64, 0, put_w)
        t0[0, pl.ds(BAND, 64), :] = turn0(w0[...])
        soft_rows(t0, 1, 64, 0, put_w)
        s[...] = turn0(w0[...])
        swap0(name, s, r)
        background()
        arrived(name, r)

        def put_r(k, v):
            q0[0, pl.ds(BAND + k, 32, stride=2), :] = v

        scatter0(r, put_r)

        def finish(p, c, v):
            m0[0, pl.ds(BAND + c, 16), :] = other[pl.ds(c, 16), :] - v

        soft_rows(q0, 1, 64, 0, finish)

    m1, t1, q1, w1 = ref["m1"], ref["t1"], ref["r1"], ref["w1"]
    a1, b1 = ref["a1"], ref["b1"]

    def swap1(name, s, r):
        exchange(name, 64, g, in_group, lambda q: s.at[pl.ds(4 * q, 4)], lambda q: r.at[pl.ds(4 * q, 4)], r.at[pl.ds(0, 252)])

    def gather1(plane_rows, s):
        for a in range(2):
            for b in range(2):
                s[pl.ds(2 * b + a, 64, stride=4), :] = plane_rows(a, b)

    def scatter1(r, store):
        for a in range(2):
            for b in range(2):
                store(b, a, r[pl.ds(2 * b + a, 64, stride=4), :])

    def source1_out():
        arrived("g1", r_g1)
        for i in range(8):
            for a in range(2):
                w1[a, 16 * i : 16 * i + 16, :] = r_g1[i, 0, a]
                b1[a, 16 * i : 16 * i + 16, :] = r_g1[i, 1, a]
        gather1(lambda a, b: w1[a, pl.ds(b, 64, stride=2), :], ref["x1s"])
        swap1("x1", ref["x1s"], ref["x1r"])

    def source2_out():
        exchange(
            "s2a", 32, px, pencil,
            lambda q: src.at[:, q],
            lambda q: r_s2a.at[pl.ds(8 * q, 8)],
            r_s2a.at[pl.ds(0, 248)],
        )

    def source1_in():
        arrived("x1", ref["x1r"])

        def put(b, a, v):
            a1[b, pl.ds(a, 64, stride=2), :] = v

        scatter1(ref["x1r"], put)

    transform0("l0a", b0, source2_out)
    transform0("l0b", a0, source1_out)
    transform0("l0c", b0, lambda: None)

    g0 = m0[0, pl.ds(BAND, 64), :] * 2.0
    own = jnp.where(core == 0, g0, half(g0))
    c1, u1 = ref["c1"], ref["u1"]
    c1[0, pl.ds(BAND, 64), :] = own

    def put_u(p, c, s, v):
        u1[pl.ds(2 * c + s, 16, stride=2), :] = v

    soft_rows_copied(c1, 1, 0, 64, 1, put_u)
    c1[0, pl.ds(BAND, 64), :] = u1[...].T[:64]
    soft_rows_copied(c1, 1, 0, 64, 1, put_u)
    l1ps, l1pr = ref["l1ps"], ref["l1pr"]
    l1ps[...] = u1[...].T
    exchange("l1p", 64, g, in_group, lambda q: l1ps.at[pl.ds(2 * q, 2)], lambda q: l1pr.at[pl.ds(2 * q, 2)], l1pr.at[pl.ds(0, 126)])
    source1_in()
    arrived("l1p", l1pr)

    def finish_l1p(b):
        def put(p, c, s, v):
            m1[b, pl.ds(BAND + 2 * c + s, 16, stride=2), :] = a1[b, pl.ds(2 * c + s, 16, stride=2), :] - v

        return put

    for b in range(2):
        c1[0, pl.ds(BAND, 64), :] = l1pr[pl.ds(b, 64, stride=2), :]
        soft_rows_copied(c1, 1, 0, 64, 1, finish_l1p(b))

    def transform1(name, other, background, times=1.0):
        s, r = ref[name + "s"], ref[name + "r"]

        def put_w(p, c, v):
            w1[p, pl.ds(c, 16), :] = v

        soft_rows(m1, 2, 128, 1, put_w)
        for p in range(2):
            t1[p, pl.ds(BAND, 128), :] = w1[p].T
        soft_rows(t1, 2, 128, 1, put_w)
        for p in range(2):
            w1[p] = w1[p].T
        gather1(lambda a, b: w1[a, pl.ds(b, 64, stride=2), :], s)
        swap1(name, s, r)
        background()
        arrived(name, r)

        def put_r(b, a, v):
            q1[b, pl.ds(BAND + a, 64, stride=2), :] = v

        scatter1(r, put_r)

        def finish(p, c, v):
            m1[p, pl.ds(BAND + c, 16), :] = (other[p, pl.ds(c, 16), :] - v) * times

        soft_rows(q1, 2, 128, 1, finish)

    a2 = ref["a2"]

    def source2_in():
        arrived("s2a", r_s2a)
        for h in range(2):
            a2[h] = r_s2a[:, 128 * h : 128 * h + 128] * LOG2E

    transform1("l1a", b1, source2_in)
    transform1("l1b", a1, lambda: None)
    transform1("l1c", b1, lambda: None, 2.0)

    w2, u2, l2ps, l2pr = ref["w2"], ref["u2"], ref["l2ps"], ref["l2pr"]

    def put_w2(p, c, s, v):
        w2[pl.ds(64 * p + 2 * c + s, 16, stride=2), :] = v

    soft_rows_copied(m1, 2, pl.multiple_of(32 * zh, 32), 32, 2, put_w2)
    u2[0, pl.ds(BAND, 128), :] = w2[...].T
    w3 = ref["w3"]

    def put_w3(p, c, s, v):
        w3[0, pl.ds(2 * c + s, 16, stride=2), :] = v

    soft_rows_copied(u2, 1, 0, 128, 2, put_w3)
    for h in range(2):
        t = w3[0, 128 * h : 128 * h + 128, :].T
        for a in range(2):
            l2ps[h, pl.ds(a, 64, stride=2), :] = t[64 * a : 64 * a + 64]
    exchange(
        "l2p", 64, g, in_group,
        lambda q: l2ps.at[:, pl.ds(2 * (32 * (q % 2) + q // 2), 2)],
        lambda q: l2pr.at[:, pl.ds(BAND + 2 * q, 2)],
        l2pr.at[:, pl.ds(0, 126)],
    )
    arrived("l2p", l2pr.at[:, pl.ds(BAND, 128)])
    m2, k2, fbs, fbr = ref["m2"], ref["k2"], ref["fbs"], ref["fbr"]
    scale = 0.05 * LN2

    def put_m2(p, c, s, v):
        v = a2[p, pl.ds(2 * c + s, 16, stride=2), :] - v
        m2[p, pl.ds(BAND + 2 * c + s, 16, stride=2), :] = v
        fbs[p, pl.ds(2 * c + s, 16, stride=2), :] = v * scale

    soft_rows_copied(l2pr, 2, 0, 128, 2, put_m2)
    exchange(
        "fb", 32, px, pencil,
        lambda q: fbs.at[:, pl.ds(8 * q, 8)],
        lambda q: fbr.at[:, pl.ds(8 * q, 8)],
        fbr.at[:, pl.ds(0, 248)],
    )

    def put_w(p, c, v):
        w3[p, pl.ds(c, 16), :] = v

    def turn2(store):
        for i in range(2):
            for j in range(2):
                store(i, j, w3[j, 128 * i : 128 * i + 128, :].T)

    def put_k2(i, j, v):
        k2[i, pl.ds(BAND + 128 * j, 128), :] = v

    soft_rows(m2, 2, 256, 2, put_w)
    turn2(put_k2)
    soft_rows(k2, 2, 256, 2, put_w)
    l2s, l2r = ref["l2s"], ref["l2r"]

    def put_l2s(i, j, v):
        l2s[i, 128 * j : 128 * j + 128, :] = v

    turn2(put_l2s)

    low = px < 16
    beside = jnp.where(low, py - 1, py + 1)
    has_beside = (beside >= 0) & (beside < 8)
    exchange(
        "l2own", 32, px, pencil,
        lambda q: l2s.at[:, pl.ds(8 * q, 8)],
        lambda q: l2r.at[BAND + q],
        l2r.at[pl.ds(0, 31)],
    )
    up, down = ROUNDS.index("l2up"), ROUNDS.index("l2down")

    def to_beside(k, place):
        def one(q, carry):
            pltpu.make_async_remote_copy(
                src_ref=l2s.at[:, pl.ds(8 * q, 8)],
                dst_ref=l2r.at[place],
                send_sem=send_sem.at[k],
                recv_sem=recv_sem.at[k],
                device_id=(q, beside),
                device_id_type=MESH,
            ).start()
            return carry

        lax.fori_loop(0, 32, one, 0)

    @pl.when(has_beside & low)
    def _():
        to_beside(down, 48 + px)

    @pl.when(has_beside & jnp.logical_not(low))
    def _():
        to_beside(up, px - 16)

    arrived("fb", fbr)
    for d in range(8):
        for h in range(2):
            f_out[d, :, 128 * h : 128 * h + 128] = fbr[h, pl.ds(d, 32, stride=8), :]

    arrived("l2own", l2r.at[pl.ds(BAND, 32)])
    edge = jnp.full((BAND, 2, 8, 128), NEG, jnp.float32)

    @pl.when(py > 0)
    def _():
        arrived("l2up", l2r.at[pl.ds(0, BAND)])

    @pl.when(py == 0)
    def _():
        l2r[pl.ds(0, BAND)] = edge

    @pl.when(py < 7)
    def _():
        arrived("l2down", l2r.at[pl.ds(48, BAND)])

    @pl.when(py == 7)
    def _():
        l2r[pl.ds(48, BAND)] = edge

    def put_rows(r, h, v):
        w3[h, pl.ds(r, 8, stride=32), :] = v

    soft_major(l2r, 32, 2, put_rows)
    for h in range(2):
        cols = slice(128 * h, 128 * h + 128)
        for d in range(8):
            g_out[d, :, cols] = tgt[d, :, cols] * 0.05 - w3[h, 32 * d : 32 * d + 32, :] * scale

    @pl.when(has_beside & low)
    def _():
        sent("l2down", l2r.at[pl.ds(0, 32)])

    @pl.when(has_beside & jnp.logical_not(low))
    def _():
        sent("l2up", l2r.at[pl.ds(0, 32)])

    for name, part in leaving:
        sent(name, part)


SCRATCH = [
    ("g0s", (2, 8, 128)), ("g0r", (8, 2, 8, 128)),
    ("g1s", (2, 4, 16, 128)), ("g1r", (8, 2, 2, 16, 128)),
    ("s2ar", (256, 256)),
    ("x0s", (64, 128)), ("x0r", (64, 128)),
    ("l0as", (64, 128)), ("l0ar", (64, 128)), ("l0bs", (64, 128)), ("l0br", (64, 128)),
    ("l0cs", (64, 128)), ("l0cr", (64, 128)),
    ("x1s", (256, 128)), ("x1r", (256, 128)),
    ("l1ps", (128, 128)), ("l1pr", (128, 128)),
    ("l1as", (256, 128)), ("l1ar", (256, 128)), ("l1bs", (256, 128)), ("l1br", (256, 128)),
    ("l1cs", (256, 128)), ("l1cr", (256, 128)),
    ("l2ps", (2, 128, 128)), ("l2pr", (2, 160, 128)),
    ("l2s", (2, 256, 128)), ("l2r", (64, 2, 8, 128)),
    ("fbs", (2, 256, 128)), ("fbr", (2, 256, 128)),
    ("m0", (1, 96, 128)), ("t0", (1, 96, 128)), ("r0", (1, 96, 128)), ("w0", (64, 128)),
    ("a0", (64, 128)), ("b0", (64, 128)),
    ("m1", (2, 160, 128)), ("t1", (2, 160, 128)), ("r1", (2, 160, 128)), ("w1", (2, 128, 128)),
    ("a1", (2, 128, 128)), ("b1", (2, 128, 128)),
    ("c1", (1, 96, 128)), ("u1", (128, 128)),
    ("u2", (1, 160, 128)), ("w2", (128, 128)), ("a2", (2, 256, 128)),
    ("m2", (2, 288, 128)), ("k2", (2, 288, 128)), ("w3", (2, 256, 128)),
]


def per_device(log_source, log_target):
    shape = jax.ShapeDtypeStruct((8, 32, 256), jnp.float32)
    vmem = pl.BlockSpec(memory_space=pltpu.VMEM)
    return pl.pallas_call(
        kernel,
        out_shape=(shape, shape),
        in_specs=[vmem, vmem],
        out_specs=(vmem, vmem),
        scratch_shapes=[pltpu.VMEM(s, jnp.float32) for _, s in SCRATCH]
        + [pltpu.SemaphoreType.DMA((len(ROUNDS),)), pltpu.SemaphoreType.DMA((len(ROUNDS),))],
        compiler_params=pltpu.CompilerParams(collective_id=0, has_side_effects=True),
        name="sinkhorn",
    )(log_source, log_target)


def solution(mesh):
    return jax.shard_map(
        per_device,
        mesh=mesh,
        in_specs=(P("px", "py", None), P("px", "py", None)),
        out_specs=(P("px", "py", None), P("px", "py", None)),
        check_vma=False,
    )
```

```python
import math

import jax
import jax.numpy as jnp
from jax import lax
from jax.experimental import pallas as pl
from jax.experimental.pallas import tpu as pltpu
from jax.sharding import PartitionSpec as P

LEVELS = 3
BAND = 16
NEG = -1e30
LOG2E = 1.4426950408889634
LN2 = 0.6931471805599453
MESH = pl.DeviceIdType.MESH
HIGHEST = lax.Precision.HIGHEST


def taps_of(level):
    inverse_width = 2.0 ** (LEVELS - 1 - level) / 18.0
    return [math.exp(-float(d * d) * inverse_width) for d in range(BAND + 1)]


def coarse_taps(level):
    taps = taps_of(level)
    weights = []
    for s in range(2):
        weights.append(
            [
                sum(taps[abs(2 * D + u - s)] for u in range(2) if abs(2 * D + u - s) <= BAND)
                for D in range(-BAND // 2, BAND // 2 + 1)
            ]
        )
    return weights


def lane_lo(shape):
    return lax.broadcasted_iota(jnp.int32, shape, 1) < 64


def half(v):
    return pltpu.roll(v, 64, 1)


def mix(a, b):
    lo = lane_lo(a.shape)
    return jnp.where(lo, a, half(b)), jnp.where(lo, half(a), b)


def tree(op, xs):
    xs = list(xs)
    while len(xs) > 1:
        xs = [op(xs[i], xs[i + 1]) if i + 1 < len(xs) else xs[i] for i in range(0, len(xs), 2)]
    return xs[0]


def soft_pair(tap, taps):
    shared = tree(jnp.maximum, [tap(t) for t in range(1, 2 * BAND + 1)])
    e = {t: jnp.exp2(tap(t) - shared) for t in range(1, 2 * BAND + 1)}
    outs = []
    for k in range(2):
        mid = BAND + k
        parts = [taps[0] * e[mid]]
        parts += [taps[d] * (e[mid - d] + e[mid + d]) for d in range(1, BAND)]
        parts += [taps[BAND] * e[1 if k else 2 * BAND]]
        accs = [tree(jnp.add, parts[i::4]) for i in range(4)]
        total = (accs[0] + accs[1]) + (accs[2] + accs[3])
        last = tap((2 * BAND + 1) * k)
        m = jnp.maximum(shared, last)
        total = total * jnp.exp2(shared - m) + taps[BAND] * jnp.exp2(last - m)
        outs.append(m + jnp.log2(total))
    return outs


def soft_rows(pad, planes, n, level, store, units=4):
    taps = taps_of(level)
    size = 16 * units
    per = n // size

    def body(it, carry):
        p = it // per
        base = pl.multiple_of((it % per) * size, size)
        for u in range(units):
            c = base + 16 * u
            outs = soft_pair(lambda t, c=c: pad[p, pl.ds(c + t, 8, stride=2), :], taps)
            for k in range(2):
                store(p, c + k, outs[k])
        return carry

    lax.fori_loop(0, planes * per, body, 0)


def every2(start, count=8):
    return pl.ds(start, count, stride=2)


def soft_rows_copied(pad, planes, first, n, level, store, chunk=16):
    weights = coarse_taps(level)
    per = n // chunk

    def body(it, carry):
        p = it // per
        c = pl.multiple_of((it % per) * chunk, chunk)

        def tap(t):
            return pad[p, pl.ds(first + c + BAND // 2 + t, chunk), :]

        m = tree(jnp.maximum, [tap(t) for t in range(BAND + 1)])
        es = [jnp.exp2(tap(t) - m) for t in range(BAND + 1)]
        for s in range(2):
            total = tree(jnp.add, [weights[s][t] * es[t] for t in range(BAND + 1)])
            store(p, c, s, m + jnp.log2(total))
        return carry

    lax.fori_loop(0, planes * per, body, 0)


def soft_major(buf, n, level, store, units=4):
    taps = taps_of(level)
    size = 2 * units
    per = n // size

    def body(it, carry):
        h = it // per
        base = (it % per) * size
        for u in range(units):
            c = base + 2 * u
            outs = soft_pair(lambda t, c=c: buf[c + t, h], taps)
            for k in range(2):
                store(c + k, h, outs[k])
        return carry

    lax.fori_loop(0, 2 * per, body, 0)


def border(pad, n):
    planes, _, lanes = pad.shape
    for p in range(planes):
        pad[p, pl.ds(0, BAND), :] = jnp.full((BAND, lanes), NEG, jnp.float32)
        pad[p, pl.ds(BAND + n, BAND), :] = jnp.full((BAND, lanes), NEG, jnp.float32)


def pair_max(v, axis):
    n = v.shape[axis]
    even = lax.broadcasted_iota(jnp.int32, v.shape, axis) % 2 == 0
    other = jnp.where(even, pltpu.roll(v, n - 1, axis), pltpu.roll(v, 1, axis))
    return jnp.maximum(v, other)


def halving(rows, cols, axis, shift=0):
    i = lax.broadcasted_iota(jnp.int32, (rows, cols), 0)
    j = lax.broadcasted_iota(jnp.int32, (rows, cols), 1)
    if axis == 0:
        return (j // 2 == i).astype(jnp.float32)
    return (i // 2 + shift == j).astype(jnp.float32)


def mm(a, b):
    return jnp.dot(a, b, precision=HIGHEST, preferred_element_type=jnp.float32)


def weight_log(pos, level, n):
    taps = taps_of(level)
    total = jnp.zeros(pos.shape, jnp.float32)
    for d in range(-BAND, BAND + 1):
        inside = (pos + d >= 0) & (pos + d < n)
        total = total + jnp.where(inside, taps[abs(d)], 0.0)
    return jnp.log2(total)


ROUNDS = [
    "g0", "g1", "s2a", "x0", "l0a", "l0b", "l0c", "x1", "l1p", "l1a", "l1b", "l1c",
    "l2p", "l2own", "l2up", "l2down", "fb",
]


FAR_FIRST = sorted(
    [(x, y, z, c) for x in range(4) for y in range(4) for z in range(2) for c in range(2)][1:],
    key=lambda d: -(min(d[0], 4 - d[0]) + min(d[1], 4 - d[1]) + d[2]),
)


def kernel(src, tgt, f_out, g_out, *scratch):
    names = [name for name, _ in SCRATCH]
    ref = dict(zip(names, scratch))
    send_sem, recv_sem = scratch[-2], scratch[-1]
    px = lax.axis_index("px")
    py = lax.axis_index("py")
    zh = py // 2
    core = py % 2
    g = 2 * px + core

    barrier = pltpu.get_barrier_semaphore()

    def in_group(q):
        return (q // 2, 2 * zh + q % 2)

    for o in range(1, 32):
        pl.semaphore_signal(barrier, inc=1, device_id=((px + o) % 32, py), device_id_type=MESH)
    for o in range(1, 8):
        pl.semaphore_signal(barrier, inc=1, device_id=(px, (py + o) % 8), device_id_type=MESH)

    near = [
        [(px % 4 + d) % 4 for d in range(4)],
        [(px // 4 % 4 + d) % 4 for d in range(4)],
        [(px // 16 + d) % 2 for d in range(2)],
        [(core + d) % 2 for d in range(2)],
    ]
    leaving = []

    def exchange(name, n, me, device, src_at, dst_at, most):
        k = ROUNDS.index(name)

        def to(q):
            pltpu.make_async_remote_copy(
                src_ref=src_at(q),
                dst_ref=dst_at(me),
                send_sem=send_sem.at[k],
                recv_sem=recv_sem.at[k],
                device_id=device(q),
                device_id_type=MESH,
            ).start()

        def one(o, carry):
            to((me + o) % n)
            return carry

        if n == 64:
            for dx, dy, dz, dc in FAR_FIRST:
                to(2 * (16 * near[2][dz] + 4 * near[1][dy] + near[0][dx]) + near[3][dc])
        else:
            lax.fori_loop(1, n, one, 0)
        pltpu.make_async_copy(src_at(me), dst_at(me), recv_sem.at[k]).start()
        leaving.append((name, most))

    def arrived(name, whole):
        k = ROUNDS.index(name)
        pltpu.make_async_copy(whole, whole, recv_sem.at[k]).wait()

    def sent(name, part):
        k = ROUNDS.index(name)
        pltpu.make_async_copy(part, part, send_sem.at[k]).wait()

    def column(q):
        return (px, q)

    def pencil(q):
        return (q, py)

    def depth(q):
        return (px, 2 * q + core)

    es, ms = [], []
    for arr in (src, tgt):
        for d in range(4):
            a = arr[2 * d] * LOG2E
            b = arr[2 * d + 1] * LOG2E
            m = pair_max(pair_max(jnp.maximum(a, b), 0), 1)
            es.append(jnp.exp2(a - m) + jnp.exp2(b - m))
            ms.append(m)
    fine = mm(jnp.concatenate(es + ms, axis=0), halving(256, 128, 1))
    rows = halving(128, 256, 0)
    r1 = mm(rows, fine[256:]) * 0.25 + jnp.log2(mm(rows, fine[:256])) - 3.0
    s1 = ref["g1s"]
    for i in range(8):
        s1[i // 4, i % 4] = r1[16 * i : 16 * i + 16]
    es, ms = [], []
    for d in range(2):
        for arr in range(2):
            o = (arr * 4 + 2 * d) * 16
            a, b = r1[o : o + 16], r1[o + 16 : o + 32]
            m = pair_max(pair_max(jnp.maximum(a, b), 0), 1)
            es.append(jnp.exp2(a - m) + jnp.exp2(b - m))
            ms.append(m)

    def packed(v):
        low = mm(jnp.concatenate(v[:2], axis=0), halving(128, 128, 1))
        high = mm(jnp.concatenate(v[2:], axis=0), halving(128, 128, 1, 64))
        return mm(halving(16, 32, 0), low + high)

    r0 = packed(ms) * 0.25 + jnp.log2(packed(es)) - 3.0
    s0 = ref["g0s"]
    s0[0] = r0[:8]
    s0[1] = r0[8:]

    pl.semaphore_wait(barrier, 38)

    r_g0, r_g1, r_s2a = ref["g0r"], ref["g1r"], ref["s2ar"]
    exchange("g0", 8, py, column, lambda q: s0, lambda q: r_g0.at[q], r_g0.at[pl.ds(0, 7)])

    for name, n in (("m0", 64), ("t0", 64), ("r0", 64), ("m1", 128), ("t1", 128), ("r1", 128), ("c1", 64), ("u2", 128),
                    ("l2pr", 128), ("m2", 256), ("k2", 256)):
        border(ref[name], n)

    m0, t0, q0, w0 = ref["m0"], ref["t0"], ref["r0"], ref["w0"]

    lanes0 = lax.broadcasted_iota(jnp.int32, (64, 128), 1)
    zero0 = (
        weight_log(lax.broadcasted_iota(jnp.int32, (64, 128), 0), 0, 64)
        + weight_log(lanes0 % 64, 0, 64)
        + weight_log(2 * px + lanes0 // 64, 0, 64)
    )

    def turn0(v):
        t = jnp.concatenate([v, v], axis=0).T
        return jnp.where(lane_lo((64, 128)), t[:64], t[64:])

    def scatter0(r, store):
        a, b = mix(r[pl.ds(0, 32, stride=2), :], r[pl.ds(1, 32, stride=2), :])
        store(0, a)
        store(1, b)

    arrived("g0", r_g0)
    x0s, x0r, a0, b0 = ref["x0s"], ref["x0r"], ref["a0"], ref["b0"]
    for i in range(8):
        x0s[8 * i : 8 * i + 8, :] = r_g0[i, 0]
        b0[8 * i : 8 * i + 8, :] = r_g0[i, 1]

    def swap0(name, s, r):
        exchange(name, 32, px, pencil, lambda q: s.at[pl.ds(2 * q, 2)], lambda q: r.at[pl.ds(2 * q, 2)], r.at[pl.ds(0, 62)])

    swap0("x0", x0s, x0r)
    exchange("g1", 8, py, column, lambda q: s1.at[:, pl.ds(2 * (q % 2), 2)], lambda q: r_g1.at[q], r_g1.at[pl.ds(0, 7)])
    arrived("x0", x0r)

    def put_a0(k, v):
        a0[pl.ds(k, 32, stride=2), :] = v

    scatter0(x0r, put_a0)
    m0[0, pl.ds(BAND, 64), :] = a0[...] - zero0

    def transform0(name, other, background):
        s, r = ref[name + "s"], ref[name + "r"]

        def put_w(p, c, v):
            w0[every2(c), :] = v

        soft_rows(m0, 1, 64, 0, put_w)
        t0[0, pl.ds(BAND, 64), :] = turn0(w0[...])
        soft_rows(t0, 1, 64, 0, put_w)
        s[...] = turn0(w0[...])
        swap0(name, s, r)
        background()
        arrived(name, r)

        def put_r(k, v):
            q0[0, pl.ds(BAND + k, 32, stride=2), :] = v

        scatter0(r, put_r)

        def finish(p, c, v):
            m0[0, every2(BAND + c), :] = other[every2(c), :] - v

        soft_rows(q0, 1, 64, 0, finish)

    m1, t1, q1, w1 = ref["m1"], ref["t1"], ref["r1"], ref["w1"]
    a1, b1 = ref["a1"], ref["b1"]

    def swap1(name, s, r):
        exchange(
            name, 64, g, in_group,
            lambda q: s.at[:, pl.ds(2 * q, 2)],
            lambda q: r.at[:, pl.ds(2 * q, 2)],
            r.at[:, pl.ds(0, 126)],
        )

    def scatter1(r, store):
        for a in range(2):
            for b in range(2):
                store(b, a, r[a, every2(b, 64), :])

    def source1_out():
        arrived("g1", r_g1)
        for i in range(8):
            for a in range(2):
                ref["x1s"][a, 16 * i : 16 * i + 16, :] = r_g1[i, 0, a]
                b1[a, 16 * i : 16 * i + 16, :] = r_g1[i, 1, a]
        swap1("x1", ref["x1s"], ref["x1r"])

    def source2_out():
        exchange(
            "s2a", 32, px, pencil,
            lambda q: src.at[:, q],
            lambda q: r_s2a.at[pl.ds(8 * q, 8)],
            r_s2a.at[pl.ds(0, 248)],
        )

    def source1_in():
        arrived("x1", ref["x1r"])

        def put(b, a, v):
            a1[b, pl.ds(a, 64, stride=2), :] = v

        scatter1(ref["x1r"], put)

    transform0("l0a", b0, source2_out)
    transform0("l0b", a0, source1_out)
    transform0("l0c", b0, lambda: None)

    g0 = m0[0, pl.ds(BAND, 64), :] * 2.0
    own = jnp.where(core == 0, g0, half(g0))
    c1, u1 = ref["c1"], ref["u1"]
    c1[0, pl.ds(BAND, 64), :] = own

    def put_u(p, c, s, v):
        u1[pl.ds(2 * c + s, 16, stride=2), :] = v

    soft_rows_copied(c1, 1, 0, 64, 1, put_u)
    c1[0, pl.ds(BAND, 64), :] = u1[...].T[:64]
    soft_rows_copied(c1, 1, 0, 64, 1, put_u)
    l1ps, l1pr = ref["l1ps"], ref["l1pr"]
    l1ps[...] = u1[...].T
    exchange("l1p", 64, g, in_group, lambda q: l1ps.at[pl.ds(2 * q, 2)], lambda q: l1pr.at[pl.ds(2 * q, 2)], l1pr.at[pl.ds(0, 126)])
    source1_in()
    arrived("l1p", l1pr)

    def finish_l1p(b):
        def put(p, c, s, v):
            m1[b, pl.ds(BAND + 2 * c + s, 16, stride=2), :] = a1[b, pl.ds(2 * c + s, 16, stride=2), :] - v

        return put

    for b in range(2):
        c1[0, pl.ds(BAND, 64), :] = l1pr[pl.ds(b, 64, stride=2), :]
        soft_rows_copied(c1, 1, 0, 64, 1, finish_l1p(b))

    def transform1(name, other, background, times=1.0):
        s, r = ref[name + "s"], ref[name + "r"]

        def put_w(p, c, v):
            w1[p, every2(c), :] = v

        soft_rows(m1, 2, 128, 1, put_w)
        for p in range(2):
            t1[p, pl.ds(BAND, 128), :] = w1[p].T
        soft_rows(t1, 2, 128, 1, put_w)
        for p in range(2):
            s[p] = w1[p].T
        swap1(name, s, r)
        background()
        arrived(name, r)

        def put_r(b, a, v):
            q1[b, pl.ds(BAND + a, 64, stride=2), :] = v

        scatter1(r, put_r)

        def finish(p, c, v):
            m1[p, every2(BAND + c), :] = (other[p, every2(c), :] - v) * times

        soft_rows(q1, 2, 128, 1, finish)

    a2 = ref["a2"]

    def source2_in():
        arrived("s2a", r_s2a)
        for h in range(2):
            a2[h] = r_s2a[:, 128 * h : 128 * h + 128] * LOG2E

    transform1("l1a", b1, source2_in)
    transform1("l1b", a1, lambda: None)
    transform1("l1c", b1, lambda: None, 2.0)

    w2, u2, l2ps, l2pr = ref["w2"], ref["u2"], ref["l2ps"], ref["l2pr"]

    def put_w2(p, c, s, v):
        w2[pl.ds(64 * p + 2 * c + s, 16, stride=2), :] = v

    soft_rows_copied(m1, 2, pl.multiple_of(32 * zh, 32), 32, 2, put_w2)
    u2[0, pl.ds(BAND, 128), :] = w2[...].T
    w3 = ref["w3"]

    def put_w3(p, c, s, v):
        w3[0, pl.ds(2 * c + s, 16, stride=2), :] = v

    soft_rows_copied(u2, 1, 0, 128, 2, put_w3)
    for h in range(2):
        t = w3[0, 128 * h : 128 * h + 128, :].T
        for a in range(2):
            l2ps[h, pl.ds(a, 64, stride=2), :] = t[64 * a : 64 * a + 64]
    exchange(
        "l2p", 64, g, in_group,
        lambda q: l2ps.at[:, pl.ds(2 * (32 * (q % 2) + q // 2), 2)],
        lambda q: l2pr.at[:, pl.ds(BAND + 2 * q, 2)],
        l2pr.at[:, pl.ds(0, 126)],
    )
    arrived("l2p", l2pr.at[:, pl.ds(BAND, 128)])
    m2, k2, fbs, fbr = ref["m2"], ref["k2"], ref["fbs"], ref["fbr"]
    scale = 0.05 * LN2

    def put_m2(p, c, s, v):
        v = a2[p, pl.ds(2 * c + s, 16, stride=2), :] - v
        m2[p, pl.ds(BAND + 2 * c + s, 16, stride=2), :] = v
        fbs[p, pl.ds(2 * c + s, 16, stride=2), :] = v * scale

    soft_rows_copied(l2pr, 2, 0, 128, 2, put_m2)
    exchange(
        "fb", 32, px, pencil,
        lambda q: fbs.at[:, pl.ds(8 * q, 8)],
        lambda q: fbr.at[:, pl.ds(8 * q, 8)],
        fbr.at[:, pl.ds(0, 248)],
    )

    def put_w(p, c, v):
        w3[p, every2(c), :] = v

    def turn2(store):
        for i in range(2):
            for j in range(2):
                store(i, j, w3[j, 128 * i : 128 * i + 128, :].T)

    def put_k2(i, j, v):
        k2[i, pl.ds(BAND + 128 * j, 128), :] = v

    soft_rows(m2, 2, 256, 2, put_w)
    turn2(put_k2)
    soft_rows(k2, 2, 256, 2, put_w)
    l2s, l2r = ref["l2s"], ref["l2r"]

    def put_l2s(i, j, v):
        l2s[i, 128 * j : 128 * j + 128, :] = v

    turn2(put_l2s)

    low = px < 16
    beside = jnp.where(low, py - 1, py + 1)
    has_beside = (beside >= 0) & (beside < 8)
    exchange(
        "l2own", 32, px, pencil,
        lambda q: l2s.at[:, pl.ds(8 * q, 8)],
        lambda q: l2r.at[BAND + q],
        l2r.at[pl.ds(0, 31)],
    )
    up, down = ROUNDS.index("l2up"), ROUNDS.index("l2down")

    def to_beside(k, place):
        def one(q, carry):
            pltpu.make_async_remote_copy(
                src_ref=l2s.at[:, pl.ds(8 * q, 8)],
                dst_ref=l2r.at[place],
                send_sem=send_sem.at[k],
                recv_sem=recv_sem.at[k],
                device_id=(q, beside),
                device_id_type=MESH,
            ).start()
            return carry

        lax.fori_loop(0, 32, one, 0)

    @pl.when(has_beside & low)
    def _():
        to_beside(down, 48 + px)

    @pl.when(has_beside & jnp.logical_not(low))
    def _():
        to_beside(up, px - 16)

    arrived("fb", fbr)
    for d in range(8):
        for h in range(2):
            f_out[d, :, 128 * h : 128 * h + 128] = fbr[h, pl.ds(d, 32, stride=8), :]

    arrived("l2own", l2r.at[pl.ds(BAND, 32)])
    edge = jnp.full((BAND, 2, 8, 128), NEG, jnp.float32)

    @pl.when(py > 0)
    def _():
        arrived("l2up", l2r.at[pl.ds(0, BAND)])

    @pl.when(py == 0)
    def _():
        l2r[pl.ds(0, BAND)] = edge

    @pl.when(py < 7)
    def _():
        arrived("l2down", l2r.at[pl.ds(48, BAND)])

    @pl.when(py == 7)
    def _():
        l2r[pl.ds(48, BAND)] = edge

    def put_rows(r, h, v):
        w3[h, pl.ds(r, 8, stride=32), :] = v

    soft_major(l2r, 32, 2, put_rows)
    for h in range(2):
        cols = slice(128 * h, 128 * h + 128)
        for d in range(8):
            g_out[d, :, cols] = tgt[d, :, cols] * 0.05 - w3[h, 32 * d : 32 * d + 32, :] * scale

    @pl.when(has_beside & low)
    def _():
        sent("l2down", l2r.at[pl.ds(0, 32)])

    @pl.when(has_beside & jnp.logical_not(low))
    def _():
        sent("l2up", l2r.at[pl.ds(0, 32)])

    for name, part in leaving:
        sent(name, part)


SCRATCH = [
    ("g0s", (2, 8, 128)), ("g0r", (8, 2, 8, 128)),
    ("g1s", (2, 4, 16, 128)), ("g1r", (8, 2, 2, 16, 128)),
    ("s2ar", (256, 256)),
    ("x0s", (64, 128)), ("x0r", (64, 128)),
    ("l0as", (64, 128)), ("l0ar", (64, 128)), ("l0bs", (64, 128)), ("l0br", (64, 128)),
    ("l0cs", (64, 128)), ("l0cr", (64, 128)),
    ("x1s", (2, 128, 128)), ("x1r", (2, 128, 128)),
    ("l1ps", (128, 128)), ("l1pr", (128, 128)),
    ("l1as", (2, 128, 128)), ("l1ar", (2, 128, 128)), ("l1bs", (2, 128, 128)), ("l1br", (2, 128, 128)),
    ("l1cs", (2, 128, 128)), ("l1cr", (2, 128, 128)),
    ("l2ps", (2, 128, 128)), ("l2pr", (2, 160, 128)),
    ("l2s", (2, 256, 128)), ("l2r", (64, 2, 8, 128)),
    ("fbs", (2, 256, 128)), ("fbr", (2, 256, 128)),
    ("m0", (1, 96, 128)), ("t0", (1, 96, 128)), ("r0", (1, 96, 128)), ("w0", (64, 128)),
    ("a0", (64, 128)), ("b0", (64, 128)),
    ("m1", (2, 160, 128)), ("t1", (2, 160, 128)), ("r1", (2, 160, 128)), ("w1", (2, 128, 128)),
    ("a1", (2, 128, 128)), ("b1", (2, 128, 128)),
    ("c1", (1, 96, 128)), ("u1", (128, 128)),
    ("u2", (1, 160, 128)), ("w2", (128, 128)), ("a2", (2, 256, 128)),
    ("m2", (2, 288, 128)), ("k2", (2, 288, 128)), ("w3", (2, 256, 128)),
]


def per_device(log_source, log_target):
    shape = jax.ShapeDtypeStruct((8, 32, 256), jnp.float32)
    vmem = pl.BlockSpec(memory_space=pltpu.VMEM)
    return pl.pallas_call(
        kernel,
        out_shape=(shape, shape),
        in_specs=[vmem, vmem],
        out_specs=(vmem, vmem),
        scratch_shapes=[pltpu.VMEM(s, jnp.float32) for _, s in SCRATCH]
        + [pltpu.SemaphoreType.DMA((len(ROUNDS),)), pltpu.SemaphoreType.DMA((len(ROUNDS),))],
        compiler_params=pltpu.CompilerParams(collective_id=0, has_side_effects=True),
        name="sinkhorn",
    )(log_source, log_target)


def solution(mesh):
    return jax.shard_map(
        per_device,
        mesh=mesh,
        in_specs=(P("px", "py", None), P("px", "py", None)),
        out_specs=(P("px", "py", None), P("px", "py", None)),
        check_vma=False,
    )
```

```python
import functools
import math

import jax
import jax.numpy as jnp
from jax import lax
from jax.experimental import pallas as pl
from jax.experimental.pallas import tpu as pltpu
from jax.sharding import PartitionSpec as P

LEVELS = 3
BAND = 16
NEG = -1e30
LOG2E = 1.4426950408889634
LN2 = 0.6931471805599453
MESH = pl.DeviceIdType.MESH
HIGHEST = lax.Precision.HIGHEST


def taps_of(level):
    inverse_width = 2.0 ** (LEVELS - 1 - level) / 18.0
    return [math.exp(-float(d * d) * inverse_width) for d in range(BAND + 1)]


def coarse_taps(level):
    taps = taps_of(level)
    weights = []
    for s in range(2):
        weights.append(
            [
                sum(taps[abs(2 * D + u - s)] for u in range(2) if abs(2 * D + u - s) <= BAND)
                for D in range(-BAND // 2, BAND // 2 + 1)
            ]
        )
    return weights


def lane_lo(shape):
    return lax.broadcasted_iota(jnp.int32, shape, 1) < 64


def half(v):
    return pltpu.roll(v, 64, 1)


def mix(a, b):
    lo = lane_lo(a.shape)
    return jnp.where(lo, a, half(b)), jnp.where(lo, half(a), b)


def tree(op, xs):
    xs = list(xs)
    while len(xs) > 1:
        xs = [op(xs[i], xs[i + 1]) if i + 1 < len(xs) else xs[i] for i in range(0, len(xs), 2)]
    return xs[0]


def soft_pair(tap, taps):
    shared = tree(jnp.maximum, [tap(t) for t in range(1, 2 * BAND + 1)])
    e = {t: jnp.exp2(tap(t) - shared) for t in range(1, 2 * BAND + 1)}
    outs = []
    for k in range(2):
        mid = BAND + k
        parts = [taps[0] * e[mid]]
        parts += [taps[d] * (e[mid - d] + e[mid + d]) for d in range(1, BAND)]
        parts += [taps[BAND] * e[1 if k else 2 * BAND]]
        accs = [tree(jnp.add, parts[i::4]) for i in range(4)]
        total = (accs[0] + accs[1]) + (accs[2] + accs[3])
        last = tap((2 * BAND + 1) * k)
        m = jnp.maximum(shared, last)
        total = total * jnp.exp2(shared - m) + taps[BAND] * jnp.exp2(last - m)
        outs.append(m + jnp.log2(total))
    return outs


def soft_rows(pad, planes, n, level, store, units=4):
    taps = taps_of(level)
    size = 16 * units
    per = n // size

    def body(it, carry):
        p = it // per
        base = pl.multiple_of((it % per) * size, size)
        for u in range(units):
            c = base + 16 * u
            outs = soft_pair(lambda t, c=c: pad[p, pl.ds(c + t, 8, stride=2), :], taps)
            for k in range(2):
                store(p, c + k, outs[k])
        return carry

    lax.fori_loop(0, planes * per, body, 0)


def every2(start, count=8):
    return pl.ds(start, count, stride=2)


def soft_rows_copied(pad, planes, first, n, level, store, chunk=16):
    weights = coarse_taps(level)
    per = n // chunk

    def body(it, carry):
        p = it // per
        c = pl.multiple_of((it % per) * chunk, chunk)

        def tap(t):
            return pad[p, pl.ds(first + c + BAND // 2 + t, chunk), :]

        m = tree(jnp.maximum, [tap(t) for t in range(BAND + 1)])
        es = [jnp.exp2(tap(t) - m) for t in range(BAND + 1)]
        for s in range(2):
            total = tree(jnp.add, [weights[s][t] * es[t] for t in range(BAND + 1)])
            store(p, c, s, m + jnp.log2(total))
        return carry

    lax.fori_loop(0, planes * per, body, 0)


def soft_major(buf, n, level, store, units=4):
    taps = taps_of(level)
    size = 2 * units
    per = n // size

    def body(it, carry):
        h = it // per
        base = (it % per) * size
        for u in range(units):
            c = base + 2 * u
            outs = soft_pair(lambda t, c=c: buf[c + t, h], taps)
            for k in range(2):
                store(c + k, h, outs[k])
        return carry

    lax.fori_loop(0, 2 * per, body, 0)


def border(pad, n):
    planes, _, lanes = pad.shape
    for p in range(planes):
        pad[p, pl.ds(0, BAND), :] = jnp.full((BAND, lanes), NEG, jnp.float32)
        pad[p, pl.ds(BAND + n, BAND), :] = jnp.full((BAND, lanes), NEG, jnp.float32)


def pair_max(v, axis):
    n = v.shape[axis]
    even = lax.broadcasted_iota(jnp.int32, v.shape, axis) % 2 == 0
    other = jnp.where(even, pltpu.roll(v, n - 1, axis), pltpu.roll(v, 1, axis))
    return jnp.maximum(v, other)


def halving(rows, cols, axis, shift=0):
    i = lax.broadcasted_iota(jnp.int32, (rows, cols), 0)
    j = lax.broadcasted_iota(jnp.int32, (rows, cols), 1)
    if axis == 0:
        return (j // 2 == i).astype(jnp.float32)
    return (i // 2 + shift == j).astype(jnp.float32)


def mm(a, b):
    return jnp.dot(a, b, precision=HIGHEST, preferred_element_type=jnp.float32)


def weight_log(pos, level, n):
    taps = taps_of(level)
    total = jnp.zeros(pos.shape, jnp.float32)
    for d in range(-BAND, BAND + 1):
        inside = (pos + d >= 0) & (pos + d < n)
        total = total + jnp.where(inside, taps[abs(d)], 0.0)
    return jnp.log2(total)


ROUNDS = [
    "g0", "g1", "s2a", "x0", "l0a", "l0b", "l0c", "x1", "l1p", "l1a", "l1b", "l1c",
    "l2p", "l2own", "l2up", "l2down", "fb",
]


FAR_FIRST = sorted(
    [(x, y, z, c) for x in range(4) for y in range(4) for z in range(2) for c in range(2)][1:],
    key=lambda d: -(min(d[0], 4 - d[0]) + min(d[1], 4 - d[1]) + d[2]),
)


def kernel(src, tgt, f_out, g_out, *scratch):
    names = [name for name, _ in SCRATCH]
    ref = dict(zip(names, scratch))
    send_sem, recv_sem = scratch[-2], scratch[-1]
    px = lax.axis_index("px")
    py = lax.axis_index("py")
    zh = py // 2
    core = py % 2
    g = 2 * px + core
    z = 2 * zh + px // 16
    own = 16 * core + px % 16

    barrier = pltpu.get_barrier_semaphore()

    def in_group(q):
        return (q // 2, 2 * zh + q % 2)

    def greet(x, y):
        pl.semaphore_signal(barrier, inc=1, device_id=(x, y), device_id_type=MESH)

    for o in range(1, 32):
        greet((px + o) % 32, own // 4)
    for o in range(1, 8):
        greet(own, (py + o) % 8)

    @pl.when(own // 4 != py)
    def _():
        greet(px, own // 4)

    @pl.when(own != px)
    def _():
        greet(own, py)

    near = [
        [(px % 4 + d) % 4 for d in range(4)],
        [(px // 4 % 4 + d) % 4 for d in range(4)],
        [(px // 16 + d) % 2 for d in range(2)],
        [(core + d) % 2 for d in range(2)],
    ]
    leaving = []

    def exchange(name, n, me, device, src_at, dst_at, most):
        k = ROUNDS.index(name)

        def to(q):
            pltpu.make_async_remote_copy(
                src_ref=src_at(q),
                dst_ref=dst_at(me),
                send_sem=send_sem.at[k],
                recv_sem=recv_sem.at[k],
                device_id=device(q),
                device_id_type=MESH,
            ).start()

        def one(o, carry):
            to((me + o) % n)
            return carry

        if device is plane:
            for dx, dy, dz, dc in FAR_FIRST:
                if dz == 0:
                    to(16 * near[3][dc] + 4 * near[1][dy] + near[0][dx])
        elif n == 64:
            for dx, dy, dz, dc in FAR_FIRST:
                to(2 * (16 * near[2][dz] + 4 * near[1][dy] + near[0][dx]) + near[3][dc])
        else:
            lax.fori_loop(1, n, one, 0)
        pltpu.make_async_copy(src_at(me), dst_at(me), recv_sem.at[k]).start()
        leaving.append((name, most))

    def arrived(name, whole):
        k = ROUNDS.index(name)
        pltpu.make_async_copy(whole, whole, recv_sem.at[k]).wait()

    def sent(name, part):
        k = ROUNDS.index(name)
        pltpu.make_async_copy(part, part, send_sem.at[k]).wait()

    def column(q):
        return (px, q)

    def plane(q):
        return (16 * (px // 16) + q % 16, 2 * zh + q // 16)

    def pencil(q):
        return (q, py)

    es, ms = [], []
    for arr in (src, tgt):
        for d in range(4):
            a = arr[2 * d] * LOG2E
            b = arr[2 * d + 1] * LOG2E
            m = pair_max(pair_max(jnp.maximum(a, b), 0), 1)
            es.append(jnp.exp2(a - m) + jnp.exp2(b - m))
            ms.append(m)
    fine = mm(jnp.concatenate(es + ms, axis=0), halving(256, 128, 1))
    rows = halving(128, 256, 0)
    r1 = mm(rows, fine[256:]) * 0.25 + jnp.log2(mm(rows, fine[:256])) - 3.0
    s1 = ref["g1s"]
    for i in range(8):
        s1[i // 4, i % 4] = r1[16 * i : 16 * i + 16]
    es, ms = [], []
    for d in range(2):
        for arr in range(2):
            o = (arr * 4 + 2 * d) * 16
            a, b = r1[o : o + 16], r1[o + 16 : o + 32]
            m = pair_max(pair_max(jnp.maximum(a, b), 0), 1)
            es.append(jnp.exp2(a - m) + jnp.exp2(b - m))
            ms.append(m)

    def packed(v):
        low = mm(jnp.concatenate(v[:2], axis=0), halving(128, 128, 1))
        high = mm(jnp.concatenate(v[2:], axis=0), halving(128, 128, 1, 64))
        return mm(halving(16, 32, 0), low + high)

    r0 = packed(ms) * 0.25 + jnp.log2(packed(es)) - 3.0
    s0 = ref["g0s"]
    s0[0] = r0[:8]
    s0[1] = r0[8:]

    own_source = (own // 4 == py).astype(jnp.int32)
    own_target = (own == px).astype(jnp.int32)
    pl.semaphore_wait(barrier, 40 - own_source - own_target)

    r_g1, r_s2a = ref["g1r"], ref["s2ar"]
    x0r, a0, b0 = ref["x0r"], ref["a0"], ref["b0"]
    k_x0, k_g0 = ROUNDS.index("x0"), ROUNDS.index("g0")

    def first_send(k, part, place, x, y):
        pltpu.make_async_remote_copy(
            src_ref=part,
            dst_ref=place,
            send_sem=send_sem.at[k],
            recv_sem=recv_sem.at[k],
            device_id=(x, y),
            device_id_type=MESH,
        ).start()

    def first_own(k, part, place):
        pltpu.make_async_copy(part, place, recv_sem.at[k]).start()

    for o in (4, 3, 5, 2, 6, 1, 7, 0):
        to_z = (z + o) % 8
        for r in range(4):
            p = 4 * py + r
            x, y = 16 * (to_z % 2) + p % 16, 2 * (to_z // 2) + p // 16
            part, place = s0.at[0, pl.ds(2 * r, 2)], x0r.at[pl.ds(2 * px, 2)]
            if o:
                first_send(k_x0, part, place, x, y)
            else:
                pl.when(p != own)(functools.partial(first_send, k_x0, part, place, x, y))
                pl.when(p == own)(functools.partial(first_own, k_x0, part, place))
    for o in (4, 3, 5, 2, 6, 1, 7, 0):
        to_z = (z + o) % 8
        x, y = 16 * (to_z % 2) + px % 16, 2 * (to_z // 2) + px // 16
        part, place = s0.at[1], b0.at[pl.ds(8 * py, 8)]
        if o:
            first_send(k_g0, part, place, x, y)
        else:
            pl.when(own != px)(functools.partial(first_send, k_g0, part, place, x, y))
            pl.when(own == px)(functools.partial(first_own, k_g0, part, place))

    for name, n in (("m0", 64), ("t0", 64), ("r0", 64), ("m1", 128), ("t1", 128), ("r1", 128), ("c1", 64), ("u2", 128),
                    ("l2pr", 128), ("m2", 256), ("k2", 256)):
        border(ref[name], n)

    m0, t0, q0, w0 = ref["m0"], ref["t0"], ref["r0"], ref["w0"]

    lanes0 = lax.broadcasted_iota(jnp.int32, (64, 128), 1)
    zero0 = (
        weight_log(lax.broadcasted_iota(jnp.int32, (64, 128), 0), 0, 64)
        + weight_log(lanes0 % 64, 0, 64)
        + weight_log(2 * own + lanes0 // 64, 0, 64)
    )

    def turn0(v):
        t = jnp.concatenate([v, v], axis=0).T
        return jnp.where(lane_lo((64, 128)), t[:64], t[64:])

    def scatter0(r, store):
        a, b = mix(r[pl.ds(0, 32, stride=2), :], r[pl.ds(1, 32, stride=2), :])
        store(0, a)
        store(1, b)

    def swap0(name, s, r):
        exchange(
            name, 32, own, plane,
            lambda q: s.at[pl.ds(2 * q, 2)],
            lambda q: r.at[pl.ds(2 * q, 2)],
            r.at[pl.ds(0, 62)],
        )

    arrived("x0", x0r)

    def put_a0(k, v):
        a0[pl.ds(k, 32, stride=2), :] = v

    scatter0(x0r, put_a0)
    m0[0, pl.ds(BAND, 64), :] = a0[...] - zero0

    def transform0(name, other, background):
        s, r = ref[name + "s"], ref[name + "r"]

        def put_w(p, c, v):
            w0[every2(c), :] = v

        soft_rows(m0, 1, 64, 0, put_w)
        t0[0, pl.ds(BAND, 64), :] = turn0(w0[...])
        soft_rows(t0, 1, 64, 0, put_w)
        s[...] = turn0(w0[...])
        swap0(name, s, r)
        background()
        arrived(name, r)

        def put_r(k, v):
            q0[0, pl.ds(BAND + k, 32, stride=2), :] = v

        scatter0(r, put_r)

        def finish(p, c, v):
            m0[0, every2(BAND + c), :] = other[every2(c), :] - v

        soft_rows(q0, 1, 64, 0, finish)

    m1, t1, q1, w1 = ref["m1"], ref["t1"], ref["r1"], ref["w1"]
    a1, b1 = ref["a1"], ref["b1"]

    def swap1(name, s, r):
        exchange(
            name, 64, g, in_group,
            lambda q: s.at[:, pl.ds(2 * q, 2)],
            lambda q: r.at[:, pl.ds(2 * q, 2)],
            r.at[:, pl.ds(0, 126)],
        )

    def scatter1(r, store):
        for a in range(2):
            for b in range(2):
                store(b, a, r[a, every2(b, 64), :])

    def source1_out():
        arrived("g1", r_g1)
        for i in range(8):
            for a in range(2):
                ref["x1s"][a, 16 * i : 16 * i + 16, :] = r_g1[i, 0, a]
                b1[a, 16 * i : 16 * i + 16, :] = r_g1[i, 1, a]
        swap1("x1", ref["x1s"], ref["x1r"])

    def source2_out():
        exchange(
            "s2a", 32, px, pencil,
            lambda q: src.at[:, q],
            lambda q: r_s2a.at[pl.ds(8 * q, 8)],
            r_s2a.at[pl.ds(0, 248)],
        )

    def source1_in():
        arrived("x1", ref["x1r"])

        def put(b, a, v):
            a1[b, pl.ds(a, 64, stride=2), :] = v

        scatter1(ref["x1r"], put)

    def first_background():
        exchange(
            "g1", 8, py, column,
            lambda q: s1.at[:, pl.ds(2 * (q % 2), 2)],
            lambda q: r_g1.at[q],
            r_g1.at[pl.ds(0, 7)],
        )
        source2_out()
        arrived("g0", b0)

    transform0("l0a", b0, first_background)
    transform0("l0b", a0, source1_out)
    transform0("l0c", b0, lambda: None)

    g0 = m0[0, pl.ds(BAND, 64), :] * 2.0
    mine = jnp.where(px < 16, g0, half(g0))
    c1, u1 = ref["c1"], ref["u1"]
    c1[0, pl.ds(BAND, 64), :] = mine

    def put_u(p, c, s, v):
        u1[pl.ds(2 * c + s, 16, stride=2), :] = v

    soft_rows_copied(c1, 1, 0, 64, 1, put_u)
    c1[0, pl.ds(BAND, 64), :] = u1[...].T[:64]
    soft_rows_copied(c1, 1, 0, 64, 1, put_u)
    l1ps, l1pr = ref["l1ps"], ref["l1pr"]
    l1ps[...] = u1[...].T
    coarse = 2 * own + px // 16
    exchange(
        "l1p", 64, g, in_group,
        lambda q: l1ps.at[pl.ds(2 * q, 2)],
        lambda q: l1pr.at[pl.ds(2 * coarse, 2)],
        l1pr.at[pl.ds(0, 126)],
    )
    source1_in()
    arrived("l1p", l1pr)

    def finish_l1p(b):
        def put(p, c, s, v):
            m1[b, pl.ds(BAND + 2 * c + s, 16, stride=2), :] = a1[b, pl.ds(2 * c + s, 16, stride=2), :] - v

        return put

    for b in range(2):
        c1[0, pl.ds(BAND, 64), :] = l1pr[pl.ds(b, 64, stride=2), :]
        soft_rows_copied(c1, 1, 0, 64, 1, finish_l1p(b))

    def transform1(name, other, background, times=1.0):
        s, r = ref[name + "s"], ref[name + "r"]

        def put_w(p, c, v):
            w1[p, every2(c), :] = v

        soft_rows(m1, 2, 128, 1, put_w)
        for p in range(2):
            t1[p, pl.ds(BAND, 128), :] = w1[p].T
        soft_rows(t1, 2, 128, 1, put_w)
        for p in range(2):
            s[p] = w1[p].T
        swap1(name, s, r)
        background()
        arrived(name, r)

        def put_r(b, a, v):
            q1[b, pl.ds(BAND + a, 64, stride=2), :] = v

        scatter1(r, put_r)

        def finish(p, c, v):
            m1[p, every2(BAND + c), :] = (other[p, every2(c), :] - v) * times

        soft_rows(q1, 2, 128, 1, finish)

    a2 = ref["a2"]

    def source2_in():
        arrived("s2a", r_s2a)
        for h in range(2):
            a2[h] = r_s2a[:, 128 * h : 128 * h + 128] * LOG2E

    transform1("l1a", b1, source2_in)
    transform1("l1b", a1, lambda: None)
    transform1("l1c", b1, lambda: None, 2.0)

    w2, u2, l2ps, l2pr = ref["w2"], ref["u2"], ref["l2ps"], ref["l2pr"]

    def put_w2(p, c, s, v):
        w2[pl.ds(64 * p + 2 * c + s, 16, stride=2), :] = v

    soft_rows_copied(m1, 2, pl.multiple_of(32 * zh, 32), 32, 2, put_w2)
    u2[0, pl.ds(BAND, 128), :] = w2[...].T
    w3 = ref["w3"]

    def put_w3(p, c, s, v):
        w3[0, pl.ds(2 * c + s, 16, stride=2), :] = v

    soft_rows_copied(u2, 1, 0, 128, 2, put_w3)
    for h in range(2):
        t = w3[0, 128 * h : 128 * h + 128, :].T
        for a in range(2):
            l2ps[h, pl.ds(a, 64, stride=2), :] = t[64 * a : 64 * a + 64]
    exchange(
        "l2p", 64, g, in_group,
        lambda q: l2ps.at[:, pl.ds(2 * (32 * (q % 2) + q // 2), 2)],
        lambda q: l2pr.at[:, pl.ds(BAND + 2 * q, 2)],
        l2pr.at[:, pl.ds(0, 126)],
    )
    arrived("l2p", l2pr.at[:, pl.ds(BAND, 128)])
    m2, k2, fbs, fbr = ref["m2"], ref["k2"], ref["fbs"], ref["fbr"]
    scale = 0.05 * LN2

    def put_m2(p, c, s, v):
        v = a2[p, pl.ds(2 * c + s, 16, stride=2), :] - v
        m2[p, pl.ds(BAND + 2 * c + s, 16, stride=2), :] = v
        fbs[p, pl.ds(2 * c + s, 16, stride=2), :] = v * scale

    soft_rows_copied(l2pr, 2, 0, 128, 2, put_m2)
    exchange(
        "fb", 32, px, pencil,
        lambda q: fbs.at[:, pl.ds(8 * q, 8)],
        lambda q: fbr.at[:, pl.ds(8 * q, 8)],
        fbr.at[:, pl.ds(0, 248)],
    )

    def put_w(p, c, v):
        w3[p, every2(c), :] = v

    def turn2(store):
        for i in range(2):
            for j in range(2):
                store(i, j, w3[j, 128 * i : 128 * i + 128, :].T)

    def put_k2(i, j, v):
        k2[i, pl.ds(BAND + 128 * j, 128), :] = v

    soft_rows(m2, 2, 256, 2, put_w)
    turn2(put_k2)
    soft_rows(k2, 2, 256, 2, put_w)
    l2s, l2r = ref["l2s"], ref["l2r"]

    def put_l2s(i, j, v):
        l2s[i, 128 * j : 128 * j + 128, :] = v

    turn2(put_l2s)

    low = px < 16
    beside = jnp.where(low, py - 1, py + 1)
    has_beside = (beside >= 0) & (beside < 8)
    exchange(
        "l2own", 32, px, pencil,
        lambda q: l2s.at[:, pl.ds(8 * q, 8)],
        lambda q: l2r.at[BAND + q],
        l2r.at[pl.ds(0, 31)],
    )
    up, down = ROUNDS.index("l2up"), ROUNDS.index("l2down")

    def to_beside(k, place):
        def one(q, carry):
            pltpu.make_async_remote_copy(
                src_ref=l2s.at[:, pl.ds(8 * q, 8)],
                dst_ref=l2r.at[place],
                send_sem=send_sem.at[k],
                recv_sem=recv_sem.at[k],
                device_id=(q, beside),
                device_id_type=MESH,
            ).start()
            return carry

        lax.fori_loop(0, 32, one, 0)

    @pl.when(has_beside & low)
    def _():
        to_beside(down, 48 + px)

    @pl.when(has_beside & jnp.logical_not(low))
    def _():
        to_beside(up, px - 16)

    arrived("fb", fbr)
    for d in range(8):
        for h in range(2):
            f_out[d, :, 128 * h : 128 * h + 128] = fbr[h, pl.ds(d, 32, stride=8), :]

    arrived("l2own", l2r.at[pl.ds(BAND, 32)])
    edge = jnp.full((BAND, 2, 8, 128), NEG, jnp.float32)

    @pl.when(py > 0)
    def _():
        arrived("l2up", l2r.at[pl.ds(0, BAND)])

    @pl.when(py == 0)
    def _():
        l2r[pl.ds(0, BAND)] = edge

    @pl.when(py < 7)
    def _():
        arrived("l2down", l2r.at[pl.ds(48, BAND)])

    @pl.when(py == 7)
    def _():
        l2r[pl.ds(48, BAND)] = edge

    def put_rows(r, h, v):
        w3[h, pl.ds(r, 8, stride=32), :] = v

    soft_major(l2r, 32, 2, put_rows)
    for h in range(2):
        cols = slice(128 * h, 128 * h + 128)
        for d in range(8):
            g_out[d, :, cols] = tgt[d, :, cols] * 0.05 - w3[h, 32 * d : 32 * d + 32, :] * scale

    @pl.when(has_beside & low)
    def _():
        sent("l2down", l2r.at[pl.ds(0, 32)])

    @pl.when(has_beside & jnp.logical_not(low))
    def _():
        sent("l2up", l2r.at[pl.ds(0, 32)])

    for name, part in leaving:
        sent(name, part)
    sent("x0", x0r.at[pl.ds(0, 62)])
    sent("g0", b0.at[pl.ds(0, 56)])
    pl.when(own // 4 != py)(lambda: sent("x0", x0r.at[pl.ds(0, 2)]))
    pl.when(own != px)(lambda: sent("g0", b0.at[pl.ds(0, 8)]))


SCRATCH = [
    ("g0s", (2, 8, 128)),
    ("g1s", (2, 4, 16, 128)), ("g1r", (8, 2, 2, 16, 128)),
    ("s2ar", (256, 256)),
    ("x0r", (64, 128)),
    ("l0as", (64, 128)), ("l0ar", (64, 128)), ("l0bs", (64, 128)), ("l0br", (64, 128)),
    ("l0cs", (64, 128)), ("l0cr", (64, 128)),
    ("x1s", (2, 128, 128)), ("x1r", (2, 128, 128)),
    ("l1ps", (128, 128)), ("l1pr", (128, 128)),
    ("l1as", (2, 128, 128)), ("l1ar", (2, 128, 128)), ("l1bs", (2, 128, 128)), ("l1br", (2, 128, 128)),
    ("l1cs", (2, 128, 128)), ("l1cr", (2, 128, 128)),
    ("l2ps", (2, 128, 128)), ("l2pr", (2, 160, 128)),
    ("l2s", (2, 256, 128)), ("l2r", (64, 2, 8, 128)),
    ("fbs", (2, 256, 128)), ("fbr", (2, 256, 128)),
    ("m0", (1, 96, 128)), ("t0", (1, 96, 128)), ("r0", (1, 96, 128)), ("w0", (64, 128)),
    ("a0", (64, 128)), ("b0", (64, 128)),
    ("m1", (2, 160, 128)), ("t1", (2, 160, 128)), ("r1", (2, 160, 128)), ("w1", (2, 128, 128)),
    ("a1", (2, 128, 128)), ("b1", (2, 128, 128)),
    ("c1", (1, 96, 128)), ("u1", (128, 128)),
    ("u2", (1, 160, 128)), ("w2", (128, 128)), ("a2", (2, 256, 128)),
    ("m2", (2, 288, 128)), ("k2", (2, 288, 128)), ("w3", (2, 256, 128)),
]


def per_device(log_source, log_target):
    shape = jax.ShapeDtypeStruct((8, 32, 256), jnp.float32)
    vmem = pl.BlockSpec(memory_space=pltpu.VMEM)
    return pl.pallas_call(
        kernel,
        out_shape=(shape, shape),
        in_specs=[vmem, vmem],
        out_specs=(vmem, vmem),
        scratch_shapes=[pltpu.VMEM(s, jnp.float32) for _, s in SCRATCH]
        + [pltpu.SemaphoreType.DMA((len(ROUNDS),)), pltpu.SemaphoreType.DMA((len(ROUNDS),))],
        compiler_params=pltpu.CompilerParams(collective_id=0, has_side_effects=True),
        name="sinkhorn",
    )(log_source, log_target)


def solution(mesh):
    return jax.shard_map(
        per_device,
        mesh=mesh,
        in_specs=(P("px", "py", None), P("px", "py", None)),
        out_specs=(P("px", "py", None), P("px", "py", None)),
        check_vma=False,
    )
```

```python
import functools
import math

import jax
import jax.numpy as jnp
from jax import lax
from jax.experimental import pallas as pl
from jax.experimental.pallas import tpu as pltpu
from jax.sharding import PartitionSpec as P

LEVELS = 3
BAND = 16
NEG = -1e30
LOG2E = 1.4426950408889634
LN2 = 0.6931471805599453
MESH = pl.DeviceIdType.MESH
HIGHEST = lax.Precision.HIGHEST


def taps_of(level):
    inverse_width = 2.0 ** (LEVELS - 1 - level) / 18.0
    return [math.exp(-float(d * d) * inverse_width) for d in range(BAND + 1)]


def coarse_taps(level):
    taps = taps_of(level)
    weights = []
    for s in range(2):
        weights.append(
            [
                sum(taps[abs(2 * D + u - s)] for u in range(2) if abs(2 * D + u - s) <= BAND)
                for D in range(-BAND // 2, BAND // 2 + 1)
            ]
        )
    return weights


def lane_lo(shape):
    return lax.broadcasted_iota(jnp.int32, shape, 1) < 64


def half(v):
    return pltpu.roll(v, 64, 1)


def mix(a, b):
    lo = lane_lo(a.shape)
    return jnp.where(lo, a, half(b)), jnp.where(lo, half(a), b)


def tree(op, xs):
    xs = list(xs)
    while len(xs) > 1:
        xs = [op(xs[i], xs[i + 1]) if i + 1 < len(xs) else xs[i] for i in range(0, len(xs), 2)]
    return xs[0]


def soft_pair(tap, taps):
    shared = tree(jnp.maximum, [tap(t) for t in range(1, 2 * BAND + 1)])
    e = {t: jnp.exp2(tap(t) - shared) for t in range(1, 2 * BAND + 1)}
    outs = []
    for k in range(2):
        mid = BAND + k
        parts = [taps[0] * e[mid]]
        parts += [taps[d] * (e[mid - d] + e[mid + d]) for d in range(1, BAND)]
        parts += [taps[BAND] * e[1 if k else 2 * BAND]]
        accs = [tree(jnp.add, parts[i::4]) for i in range(4)]
        total = (accs[0] + accs[1]) + (accs[2] + accs[3])
        last = tap((2 * BAND + 1) * k)
        m = jnp.maximum(shared, last)
        total = total * jnp.exp2(shared - m) + taps[BAND] * jnp.exp2(last - m)
        outs.append(m + jnp.log2(total))
    return outs


def soft_rows(pad, planes, n, level, store, units=4):
    taps = taps_of(level)
    size = 16 * units
    per = n // size

    def body(it, carry):
        p = it // per
        base = pl.multiple_of((it % per) * size, size)
        for u in range(units):
            c = base + 16 * u
            outs = soft_pair(lambda t, c=c: pad[p, pl.ds(c + t, 8, stride=2), :], taps)
            for k in range(2):
                store(p, c + k, outs[k])
        return carry

    lax.fori_loop(0, planes * per, body, 0)


def every2(start, count=8):
    return pl.ds(start, count, stride=2)


def soft_rows_copied(pad, planes, first, n, level, store, chunk=16):
    weights = coarse_taps(level)
    per = n // chunk

    def body(it, carry):
        p = it // per
        c = pl.multiple_of((it % per) * chunk, chunk)

        def tap(t):
            return pad[p, pl.ds(first + c + BAND // 2 + t, chunk), :]

        m = tree(jnp.maximum, [tap(t) for t in range(BAND + 1)])
        es = [jnp.exp2(tap(t) - m) for t in range(BAND + 1)]
        for s in range(2):
            total = tree(jnp.add, [weights[s][t] * es[t] for t in range(BAND + 1)])
            store(p, c, s, m + jnp.log2(total))
        return carry

    lax.fori_loop(0, planes * per, body, 0)


def soft_major(buf, n, level, store, units=4):
    taps = taps_of(level)
    size = 2 * units
    per = n // size

    def body(it, carry):
        h = it // per
        base = (it % per) * size
        for u in range(units):
            c = base + 2 * u
            outs = soft_pair(lambda t, c=c: buf[c + t, h], taps)
            for k in range(2):
                store(c + k, h, outs[k])
        return carry

    lax.fori_loop(0, 2 * per, body, 0)


def border(pad, n):
    planes, _, lanes = pad.shape
    for p in range(planes):
        pad[p, pl.ds(0, BAND), :] = jnp.full((BAND, lanes), NEG, jnp.float32)
        pad[p, pl.ds(BAND + n, BAND), :] = jnp.full((BAND, lanes), NEG, jnp.float32)


def pair_max(v, axis):
    n = v.shape[axis]
    even = lax.broadcasted_iota(jnp.int32, v.shape, axis) % 2 == 0
    other = jnp.where(even, pltpu.roll(v, n - 1, axis), pltpu.roll(v, 1, axis))
    return jnp.maximum(v, other)


def halving(rows, cols, axis, shift=0):
    i = lax.broadcasted_iota(jnp.int32, (rows, cols), 0)
    j = lax.broadcasted_iota(jnp.int32, (rows, cols), 1)
    if axis == 0:
        return (j // 2 == i).astype(jnp.float32)
    return (i // 2 + shift == j).astype(jnp.float32)


def mm(a, b):
    return jnp.dot(a, b, precision=HIGHEST, preferred_element_type=jnp.float32)


def weight_log(pos, level, n):
    taps = taps_of(level)
    total = jnp.zeros(pos.shape, jnp.float32)
    for d in range(-BAND, BAND + 1):
        inside = (pos + d >= 0) & (pos + d < n)
        total = total + jnp.where(inside, taps[abs(d)], 0.0)
    return jnp.log2(total)


ROUNDS = [
    "g0", "g1", "s2a", "x0", "l0a", "l0b", "l0c", "x1", "l1p", "l1a", "l1b", "l1c",
    "l2p", "l2own", "l2up", "l2down", "fb",
]


FAR_FIRST = sorted(
    [(x, y, z, c) for x in range(4) for y in range(4) for z in range(2) for c in range(2)][1:],
    key=lambda d: -(min(d[0], 4 - d[0]) + min(d[1], 4 - d[1]) + d[2]),
)


def kernel(src_in, tgt_in, f_into, g_into, *scratch):
    names = [name for name, _ in SCRATCH]
    ref = dict(zip(names, scratch))
    io_sem, send_sem, recv_sem = scratch[-3:]
    src, tgt, f_out, g_out = ref["src"], ref["tgt"], ref["f"], ref["g"]
    read_src = pltpu.make_async_copy(src_in, src, io_sem.at[0])
    read_tgt = pltpu.make_async_copy(tgt_in, tgt, io_sem.at[1])
    read_src.start()
    read_tgt.start()
    px = lax.axis_index("px")
    py = lax.axis_index("py")
    zh = py // 2
    core = py % 2
    g = 2 * px + core
    z = 2 * zh + px // 16
    own = 16 * core + px % 16

    barrier = pltpu.get_barrier_semaphore()

    def in_group(q):
        return (q // 2, 2 * zh + q % 2)

    def greet(x, y):
        pl.semaphore_signal(barrier, inc=1, device_id=(x, y), device_id_type=MESH)

    for o in range(1, 32):
        greet((px + o) % 32, own // 4)
    for o in range(1, 8):
        greet(own, (py + o) % 8)

    @pl.when(own // 4 != py)
    def _():
        greet(px, own // 4)

    @pl.when(own != px)
    def _():
        greet(own, py)

    near = [
        [(px % 4 + d) % 4 for d in range(4)],
        [(px // 4 % 4 + d) % 4 for d in range(4)],
        [(px // 16 + d) % 2 for d in range(2)],
        [(core + d) % 2 for d in range(2)],
    ]
    leaving = []

    def exchange(name, n, me, device, src_at, dst_at, most):
        k = ROUNDS.index(name)

        def to(q):
            pltpu.make_async_remote_copy(
                src_ref=src_at(q),
                dst_ref=dst_at(me),
                send_sem=send_sem.at[k],
                recv_sem=recv_sem.at[k],
                device_id=device(q),
                device_id_type=MESH,
            ).start()

        def one(o, carry):
            to((me + o) % n)
            return carry

        if device is plane:
            for dx, dy, dz, dc in FAR_FIRST:
                if dz == 0:
                    to(16 * near[3][dc] + 4 * near[1][dy] + near[0][dx])
        elif n == 64:
            for dx, dy, dz, dc in FAR_FIRST:
                to(2 * (16 * near[2][dz] + 4 * near[1][dy] + near[0][dx]) + near[3][dc])
        else:
            lax.fori_loop(1, n, one, 0)
        pltpu.make_async_copy(src_at(me), dst_at(me), recv_sem.at[k]).start()
        leaving.append((name, most))

    def arrived(name, whole):
        k = ROUNDS.index(name)
        pltpu.make_async_copy(whole, whole, recv_sem.at[k]).wait()

    def sent(name, part):
        k = ROUNDS.index(name)
        pltpu.make_async_copy(part, part, send_sem.at[k]).wait()

    def column(q):
        return (px, q)

    def plane(q):
        return (16 * (px // 16) + q % 16, 2 * zh + q // 16)

    def pencil(q):
        return (q, py)

    for name, n in (("m0", 64), ("t0", 64), ("r0", 64), ("m1", 128), ("t1", 128), ("r1", 128), ("c1", 64), ("u2", 128),
                    ("l2pr", 128), ("m2", 256), ("k2", 256)):
        border(ref[name], n)

    read_src.wait()
    read_tgt.wait()
    es, ms = [], []
    for arr in (src, tgt):
        for d in range(4):
            a = arr[2 * d] * LOG2E
            b = arr[2 * d + 1] * LOG2E
            m = pair_max(pair_max(jnp.maximum(a, b), 0), 1)
            es.append(jnp.exp2(a - m) + jnp.exp2(b - m))
            ms.append(m)
    fine = mm(jnp.concatenate(es + ms, axis=0), halving(256, 128, 1))
    rows = halving(128, 256, 0)
    r1 = mm(rows, fine[256:]) * 0.25 + jnp.log2(mm(rows, fine[:256])) - 3.0
    s1 = ref["g1s"]
    for i in range(8):
        s1[i // 4, i % 4] = r1[16 * i : 16 * i + 16]
    es, ms = [], []
    for d in range(2):
        for arr in range(2):
            o = (arr * 4 + 2 * d) * 16
            a, b = r1[o : o + 16], r1[o + 16 : o + 32]
            m = pair_max(pair_max(jnp.maximum(a, b), 0), 1)
            es.append(jnp.exp2(a - m) + jnp.exp2(b - m))
            ms.append(m)

    def packed(v):
        low = mm(jnp.concatenate(v[:2], axis=0), halving(128, 128, 1))
        high = mm(jnp.concatenate(v[2:], axis=0), halving(128, 128, 1, 64))
        return mm(halving(16, 32, 0), low + high)

    r0 = packed(ms) * 0.25 + jnp.log2(packed(es)) - 3.0
    s0 = ref["g0s"]
    s0[0] = r0[:8]
    s0[1] = r0[8:]

    own_source = (own // 4 == py).astype(jnp.int32)
    own_target = (own == px).astype(jnp.int32)
    pl.semaphore_wait(barrier, 40 - own_source - own_target)

    r_g1, r_s2a = ref["g1r"], ref["s2ar"]
    x0r, a0, b0 = ref["x0r"], ref["a0"], ref["b0"]
    k_x0, k_g0 = ROUNDS.index("x0"), ROUNDS.index("g0")

    def first_send(k, part, place, x, y):
        pltpu.make_async_remote_copy(
            src_ref=part,
            dst_ref=place,
            send_sem=send_sem.at[k],
            recv_sem=recv_sem.at[k],
            device_id=(x, y),
            device_id_type=MESH,
        ).start()

    def first_own(k, part, place):
        pltpu.make_async_copy(part, place, recv_sem.at[k]).start()

    for o in (4, 3, 5, 2, 6, 1, 7, 0):
        to_z = (z + o) % 8
        for r in range(4):
            p = 4 * py + r
            x, y = 16 * (to_z % 2) + p % 16, 2 * (to_z // 2) + p // 16
            part, place = s0.at[0, pl.ds(2 * r, 2)], x0r.at[pl.ds(2 * px, 2)]
            if o:
                first_send(k_x0, part, place, x, y)
            else:
                pl.when(p != own)(functools.partial(first_send, k_x0, part, place, x, y))
                pl.when(p == own)(functools.partial(first_own, k_x0, part, place))
    for o in (4, 3, 5, 2, 6, 1, 7, 0):
        to_z = (z + o) % 8
        x, y = 16 * (to_z % 2) + px % 16, 2 * (to_z // 2) + px // 16
        part, place = s0.at[1], b0.at[pl.ds(8 * py, 8)]
        if o:
            first_send(k_g0, part, place, x, y)
        else:
            pl.when(own != px)(functools.partial(first_send, k_g0, part, place, x, y))
            pl.when(own == px)(functools.partial(first_own, k_g0, part, place))

    m0, t0, q0, w0 = ref["m0"], ref["t0"], ref["r0"], ref["w0"]

    lanes0 = lax.broadcasted_iota(jnp.int32, (64, 128), 1)
    zero0 = (
        weight_log(lax.broadcasted_iota(jnp.int32, (64, 128), 0), 0, 64)
        + weight_log(lanes0 % 64, 0, 64)
        + weight_log(2 * own + lanes0 // 64, 0, 64)
    )

    def turn0(v):
        t = jnp.concatenate([v, v], axis=0).T
        return jnp.where(lane_lo((64, 128)), t[:64], t[64:])

    def scatter0(r, store):
        a, b = mix(r[pl.ds(0, 32, stride=2), :], r[pl.ds(1, 32, stride=2), :])
        store(0, a)
        store(1, b)

    def swap0(name, s, r):
        exchange(
            name, 32, own, plane,
            lambda q: s.at[pl.ds(2 * q, 2)],
            lambda q: r.at[pl.ds(2 * q, 2)],
            r.at[pl.ds(0, 62)],
        )

    arrived("x0", x0r)

    def put_a0(k, v):
        a0[pl.ds(k, 32, stride=2), :] = v

    scatter0(x0r, put_a0)
    m0[0, pl.ds(BAND, 64), :] = a0[...] - zero0

    def transform0(name, other, background):
        s, r = ref[name + "s"], ref[name + "r"]

        def put_w(p, c, v):
            w0[every2(c), :] = v

        soft_rows(m0, 1, 64, 0, put_w)
        t0[0, pl.ds(BAND, 64), :] = turn0(w0[...])
        soft_rows(t0, 1, 64, 0, put_w)
        s[...] = turn0(w0[...])
        swap0(name, s, r)
        background()
        arrived(name, r)

        def put_r(k, v):
            q0[0, pl.ds(BAND + k, 32, stride=2), :] = v

        scatter0(r, put_r)

        def finish(p, c, v):
            m0[0, every2(BAND + c), :] = other[every2(c), :] - v

        soft_rows(q0, 1, 64, 0, finish)

    m1, t1, q1, w1 = ref["m1"], ref["t1"], ref["r1"], ref["w1"]
    a1, b1 = ref["a1"], ref["b1"]

    def swap1(name, s, r):
        exchange(
            name, 64, g, in_group,
            lambda q: s.at[:, pl.ds(2 * q, 2)],
            lambda q: r.at[:, pl.ds(2 * q, 2)],
            r.at[:, pl.ds(0, 126)],
        )

    def scatter1(r, store):
        for a in range(2):
            for b in range(2):
                store(b, a, r[a, every2(b, 64), :])

    def source1_out():
        arrived("g1", r_g1)
        for i in range(8):
            for a in range(2):
                ref["x1s"][a, 16 * i : 16 * i + 16, :] = r_g1[i, 0, a]
                b1[a, 16 * i : 16 * i + 16, :] = r_g1[i, 1, a]
        swap1("x1", ref["x1s"], ref["x1r"])

    def source2_out():
        exchange(
            "s2a", 32, px, pencil,
            lambda q: src.at[:, q],
            lambda q: r_s2a.at[pl.ds(8 * q, 8)],
            r_s2a.at[pl.ds(0, 248)],
        )

    def source1_in():
        arrived("x1", ref["x1r"])

        def put(b, a, v):
            a1[b, pl.ds(a, 64, stride=2), :] = v

        scatter1(ref["x1r"], put)

    def first_background():
        exchange(
            "g1", 8, py, column,
            lambda q: s1.at[:, pl.ds(2 * (q % 2), 2)],
            lambda q: r_g1.at[q],
            r_g1.at[pl.ds(0, 7)],
        )
        source2_out()
        arrived("g0", b0)

    transform0("l0a", b0, first_background)
    transform0("l0b", a0, source1_out)
    transform0("l0c", b0, lambda: None)

    g0 = m0[0, pl.ds(BAND, 64), :] * 2.0
    mine = jnp.where(px < 16, g0, half(g0))
    c1, u1 = ref["c1"], ref["u1"]
    c1[0, pl.ds(BAND, 64), :] = mine

    def put_u(p, c, s, v):
        u1[pl.ds(2 * c + s, 16, stride=2), :] = v

    soft_rows_copied(c1, 1, 0, 64, 1, put_u)
    c1[0, pl.ds(BAND, 64), :] = u1[...].T[:64]
    soft_rows_copied(c1, 1, 0, 64, 1, put_u)
    l1ps, l1pr = ref["l1ps"], ref["l1pr"]
    l1ps[...] = u1[...].T
    coarse = 2 * own + px // 16
    exchange(
        "l1p", 64, g, in_group,
        lambda q: l1ps.at[pl.ds(2 * q, 2)],
        lambda q: l1pr.at[pl.ds(2 * coarse, 2)],
        l1pr.at[pl.ds(0, 126)],
    )
    source1_in()
    arrived("l1p", l1pr)

    def finish_l1p(b):
        def put(p, c, s, v):
            m1[b, pl.ds(BAND + 2 * c + s, 16, stride=2), :] = a1[b, pl.ds(2 * c + s, 16, stride=2), :] - v

        return put

    for b in range(2):
        c1[0, pl.ds(BAND, 64), :] = l1pr[pl.ds(b, 64, stride=2), :]
        soft_rows_copied(c1, 1, 0, 64, 1, finish_l1p(b))

    def transform1(name, other, background, times=1.0):
        s, r = ref[name + "s"], ref[name + "r"]

        def put_w(p, c, v):
            w1[p, every2(c), :] = v

        soft_rows(m1, 2, 128, 1, put_w)
        for p in range(2):
            t1[p, pl.ds(BAND, 128), :] = w1[p].T
        soft_rows(t1, 2, 128, 1, put_w)
        for p in range(2):
            s[p] = w1[p].T
        swap1(name, s, r)
        background()
        arrived(name, r)

        def put_r(b, a, v):
            q1[b, pl.ds(BAND + a, 64, stride=2), :] = v

        scatter1(r, put_r)

        def finish(p, c, v):
            m1[p, every2(BAND + c), :] = (other[p, every2(c), :] - v) * times

        soft_rows(q1, 2, 128, 1, finish)

    a2 = ref["a2"]

    def source2_in():
        arrived("s2a", r_s2a)
        for h in range(2):
            a2[h] = r_s2a[:, 128 * h : 128 * h + 128] * LOG2E

    transform1("l1a", b1, source2_in)
    transform1("l1b", a1, lambda: None)
    transform1("l1c", b1, lambda: None, 2.0)

    w2, u2, l2ps, l2pr = ref["w2"], ref["u2"], ref["l2ps"], ref["l2pr"]

    def put_w2(p, c, s, v):
        w2[pl.ds(64 * p + 2 * c + s, 16, stride=2), :] = v

    soft_rows_copied(m1, 2, pl.multiple_of(32 * zh, 32), 32, 2, put_w2)
    u2[0, pl.ds(BAND, 128), :] = w2[...].T
    w3 = ref["w3"]

    def put_w3(p, c, s, v):
        w3[0, pl.ds(2 * c + s, 16, stride=2), :] = v

    soft_rows_copied(u2, 1, 0, 128, 2, put_w3)
    for h in range(2):
        t = w3[0, 128 * h : 128 * h + 128, :].T
        for a in range(2):
            l2ps[h, pl.ds(a, 64, stride=2), :] = t[64 * a : 64 * a + 64]
    exchange(
        "l2p", 64, g, in_group,
        lambda q: l2ps.at[:, pl.ds(2 * (32 * (q % 2) + q // 2), 2)],
        lambda q: l2pr.at[:, pl.ds(BAND + 2 * q, 2)],
        l2pr.at[:, pl.ds(0, 126)],
    )
    arrived("l2p", l2pr.at[:, pl.ds(BAND, 128)])
    m2, k2, fbr = ref["m2"], ref["k2"], ref["fbr"]

    def put_m2(p, c, s, v):
        m2[p, pl.ds(BAND + 2 * c + s, 16, stride=2), :] = a2[p, pl.ds(2 * c + s, 16, stride=2), :] - v

    soft_rows_copied(l2pr, 2, 0, 128, 2, put_m2)
    exchange(
        "fb", 32, px, pencil,
        lambda q: m2.at[:, pl.ds(BAND + 8 * q, 8)],
        lambda q: fbr.at[:, pl.ds(8 * q, 8)],
        fbr.at[:, pl.ds(0, 248)],
    )

    def put_w(p, c, v):
        w3[p, every2(c), :] = v

    def turn2(store):
        for i in range(2):
            for j in range(2):
                store(i, j, w3[j, 128 * i : 128 * i + 128, :].T)

    def put_k2(i, j, v):
        k2[i, pl.ds(BAND + 128 * j, 128), :] = v

    soft_rows(m2, 2, 256, 2, put_w)
    turn2(put_k2)
    l2s, l2r = ref["l2s"], ref["l2r"]

    low = px < 16
    beside = jnp.where(low, py - 1, py + 1)
    has_beside = (beside >= 0) & (beside < 8)
    k_own = ROUNDS.index("l2own")
    k_beside = jnp.where(low, ROUNDS.index("l2down"), ROUNDS.index("l2up"))
    place = jnp.where(low, 48 + px, px - 16)

    def last_send(k, q, row, y):
        pltpu.make_async_remote_copy(
            src_ref=l2s.at[:, pl.ds(8 * q, 8)],
            dst_ref=l2r.at[row],
            send_sem=send_sem.at[k],
            recv_sem=recv_sem.at[k],
            device_id=(q, y),
            device_id_type=MESH,
        ).start()

    def last_own():
        pltpu.make_async_copy(l2s.at[:, pl.ds(8 * px, 8)], l2r.at[BAND + px], recv_sem.at[k_own]).start()

    for i in range(2):

        def put_half(p, c, v, i=i):
            w3[i, every2(c), :] = v

        soft_rows(k2.at[pl.ds(i, 1)], 1, 256, 2, put_half)
        for h in range(2):
            l2s[h, 128 * i : 128 * i + 128, :] = w3[i, 128 * h : 128 * h + 128, :].T
        to = [16 * i + (px + o) % 16 for o in range(16)]

        def beside_half(to=to):
            for q in to:
                last_send(k_beside, q, place, beside)

        pl.when(has_beside)(beside_half)
        for q in to[1:]:
            last_send(k_own, q, BAND + px, py)
        pl.when(px // 16 != i)(functools.partial(last_send, k_own, to[0], BAND + px, py))
    last_own()
    leaving.append(("l2own", l2r.at[pl.ds(0, 31)]))

    arrived("fb", fbr)
    for d in range(8):
        for h in range(2):
            f_out[d, :, 128 * h : 128 * h + 128] = fbr[h, pl.ds(d, 32, stride=8), :]
    write_f = pltpu.make_async_copy(f_out, f_into, io_sem.at[2])
    write_f.start()

    arrived("l2own", l2r.at[pl.ds(BAND, 32)])
    edge = jnp.full((BAND, 2, 8, 128), NEG, jnp.float32)

    @pl.when(py > 0)
    def _():
        arrived("l2up", l2r.at[pl.ds(0, BAND)])

    @pl.when(py == 0)
    def _():
        l2r[pl.ds(0, BAND)] = edge

    @pl.when(py < 7)
    def _():
        arrived("l2down", l2r.at[pl.ds(48, BAND)])

    @pl.when(py == 7)
    def _():
        l2r[pl.ds(48, BAND)] = edge

    def put_rows(r, h, v):
        w3[h, pl.ds(r, 8, stride=32), :] = v

    soft_major(l2r, 32, 2, put_rows)
    for h in range(2):
        cols = slice(128 * h, 128 * h + 128)
        for d in range(8):
            g_out[d, :, cols] = w3[h, 32 * d : 32 * d + 32, :]
    write_g = pltpu.make_async_copy(g_out, g_into, io_sem.at[3])
    write_g.start()

    @pl.when(has_beside & low)
    def _():
        sent("l2down", l2r.at[pl.ds(0, 32)])

    @pl.when(has_beside & jnp.logical_not(low))
    def _():
        sent("l2up", l2r.at[pl.ds(0, 32)])

    write_f.wait()
    write_g.wait()
    for name, part in leaving:
        sent(name, part)
    sent("x0", x0r.at[pl.ds(0, 62)])
    sent("g0", b0.at[pl.ds(0, 56)])
    pl.when(own // 4 != py)(lambda: sent("x0", x0r.at[pl.ds(0, 2)]))
    pl.when(own != px)(lambda: sent("g0", b0.at[pl.ds(0, 8)]))


SCRATCH = [
    ("src", (8, 32, 256)), ("tgt", (8, 32, 256)), ("f", (8, 32, 256)), ("g", (8, 32, 256)),
    ("g0s", (2, 8, 128)),
    ("g1s", (2, 4, 16, 128)), ("g1r", (8, 2, 2, 16, 128)),
    ("s2ar", (256, 256)),
    ("x0r", (64, 128)),
    ("l0as", (64, 128)), ("l0ar", (64, 128)), ("l0bs", (64, 128)), ("l0br", (64, 128)),
    ("l0cs", (64, 128)), ("l0cr", (64, 128)),
    ("x1s", (2, 128, 128)), ("x1r", (2, 128, 128)),
    ("l1ps", (128, 128)), ("l1pr", (128, 128)),
    ("l1as", (2, 128, 128)), ("l1ar", (2, 128, 128)), ("l1bs", (2, 128, 128)), ("l1br", (2, 128, 128)),
    ("l1cs", (2, 128, 128)), ("l1cr", (2, 128, 128)),
    ("l2ps", (2, 128, 128)), ("l2pr", (2, 160, 128)),
    ("l2s", (2, 256, 128)), ("l2r", (64, 2, 8, 128)),
    ("fbr", (2, 256, 128)),
    ("m0", (1, 96, 128)), ("t0", (1, 96, 128)), ("r0", (1, 96, 128)), ("w0", (64, 128)),
    ("a0", (64, 128)), ("b0", (64, 128)),
    ("m1", (2, 160, 128)), ("t1", (2, 160, 128)), ("r1", (2, 160, 128)), ("w1", (2, 128, 128)),
    ("a1", (2, 128, 128)), ("b1", (2, 128, 128)),
    ("c1", (1, 96, 128)), ("u1", (128, 128)),
    ("u2", (1, 160, 128)), ("w2", (128, 128)), ("a2", (2, 256, 128)),
    ("m2", (2, 288, 128)), ("k2", (2, 288, 128)), ("w3", (2, 256, 128)),
]


def per_device(log_source, log_target):
    shape = jax.ShapeDtypeStruct((8, 32, 256), jnp.float32)
    anywhere = pl.BlockSpec(memory_space=pl.ANY)
    scaled_f, pulled = pl.pallas_call(
        kernel,
        out_shape=(shape, shape),
        in_specs=[anywhere, anywhere],
        out_specs=(anywhere, anywhere),
        scratch_shapes=[pltpu.VMEM(s, jnp.float32) for _, s in SCRATCH]
        + [pltpu.SemaphoreType.DMA((4,)), pltpu.SemaphoreType.DMA((len(ROUNDS),)), pltpu.SemaphoreType.DMA((len(ROUNDS),))],
        compiler_params=pltpu.CompilerParams(collective_id=0, has_side_effects=True),
        name="sinkhorn",
    )(log_source, log_target)
    return 0.05 * LN2 * scaled_f, 0.05 * log_target - 0.05 * LN2 * pulled


def solution(mesh):
    return jax.shard_map(
        per_device,
        mesh=mesh,
        in_specs=(P("px", "py", None), P("px", "py", None)),
        out_specs=(P("px", "py", None), P("px", "py", None)),
        check_vma=False,
    )
```

```python
import functools
import math

import jax
import jax.numpy as jnp
from jax import lax
from jax.experimental import pallas as pl
from jax.experimental.pallas import tpu as pltpu
from jax.sharding import PartitionSpec as P

LEVELS = 3
BAND = 16
NEG = -1e30
LOG2E = 1.4426950408889634
LN2 = 0.6931471805599453
MESH = pl.DeviceIdType.MESH
HIGHEST = lax.Precision.HIGHEST


def taps_of(level):
    inverse_width = 2.0 ** (LEVELS - 1 - level) / 18.0
    return [math.exp(-float(d * d) * inverse_width) for d in range(BAND + 1)]


def coarse_taps(level):
    taps = taps_of(level)
    weights = []
    for s in range(2):
        weights.append(
            [
                sum(taps[abs(2 * D + u - s)] for u in range(2) if abs(2 * D + u - s) <= BAND)
                for D in range(-BAND // 2, BAND // 2 + 1)
            ]
        )
    return weights


def lane_lo(shape):
    return lax.broadcasted_iota(jnp.int32, shape, 1) < 64


def half(v):
    return pltpu.roll(v, 64, 1)


def mix(a, b):
    lo = lane_lo(a.shape)
    return jnp.where(lo, a, half(b)), jnp.where(lo, half(a), b)


def tree(op, xs):
    xs = list(xs)
    while len(xs) > 1:
        xs = [op(xs[i], xs[i + 1]) if i + 1 < len(xs) else xs[i] for i in range(0, len(xs), 2)]
    return xs[0]


def soft_pair(tap, taps):
    shared = tree(jnp.maximum, [tap(t) for t in range(1, 2 * BAND + 1)])
    e = {t: jnp.exp2(tap(t) - shared) for t in range(1, 2 * BAND + 1)}
    outs = []
    for k in range(2):
        mid = BAND + k
        parts = [taps[0] * e[mid]]
        parts += [taps[d] * (e[mid - d] + e[mid + d]) for d in range(1, BAND)]
        parts += [taps[BAND] * e[1 if k else 2 * BAND]]
        accs = [tree(jnp.add, parts[i::4]) for i in range(4)]
        total = (accs[0] + accs[1]) + (accs[2] + accs[3])
        last = tap((2 * BAND + 1) * k)
        m = jnp.maximum(shared, last)
        total = total * jnp.exp2(shared - m) + taps[BAND] * jnp.exp2(last - m)
        outs.append(m + jnp.log2(total))
    return outs


def soft_rows(pad, planes, n, level, store, units=8):
    taps = taps_of(level)
    units = min(units, n // 16)
    size = 16 * units
    per = n // size

    def body(it, carry):
        p = it // per
        base = pl.multiple_of((it % per) * size, size)
        for u in range(units):
            c = base + 16 * u
            outs = soft_pair(lambda t, c=c: pad[p, pl.ds(c + t, 8, stride=2), :], taps)
            for k in range(2):
                store(p, c + k, outs[k])
        return carry

    lax.fori_loop(0, planes * per, body, 0)


def every2(start, count=8):
    return pl.ds(start, count, stride=2)


def soft_rows_copied(pad, planes, first, n, level, store, chunk=32):
    weights = coarse_taps(level)
    per = n // chunk

    def body(it, carry):
        p = it // per
        c = pl.multiple_of((it % per) * chunk, chunk)

        def tap(t):
            return pad[p, pl.ds(first + c + BAND // 2 + t, chunk), :]

        m = tree(jnp.maximum, [tap(t) for t in range(BAND + 1)])
        es = [jnp.exp2(tap(t) - m) for t in range(BAND + 1)]
        for s in range(2):
            total = tree(jnp.add, [weights[s][t] * es[t] for t in range(BAND + 1)])
            store(p, c, s, m + jnp.log2(total))
        return carry

    lax.fori_loop(0, planes * per, body, 0)


def soft_major(buf, n, level, store, units=4):
    taps = taps_of(level)
    size = 2 * units
    per = n // size

    def body(it, carry):
        h = it // per
        base = (it % per) * size
        for u in range(units):
            c = base + 2 * u
            outs = soft_pair(lambda t, c=c: buf[c + t, h], taps)
            for k in range(2):
                store(c + k, h, outs[k])
        return carry

    lax.fori_loop(0, 2 * per, body, 0)


def border(pad, n):
    planes, _, lanes = pad.shape
    for p in range(planes):
        pad[p, pl.ds(0, BAND), :] = jnp.full((BAND, lanes), NEG, jnp.float32)
        pad[p, pl.ds(BAND + n, BAND), :] = jnp.full((BAND, lanes), NEG, jnp.float32)


def pair_max(v, axis):
    n = v.shape[axis]
    even = lax.broadcasted_iota(jnp.int32, v.shape, axis) % 2 == 0
    other = jnp.where(even, pltpu.roll(v, n - 1, axis), pltpu.roll(v, 1, axis))
    return jnp.maximum(v, other)


def halving(rows, cols, axis, shift=0):
    i = lax.broadcasted_iota(jnp.int32, (rows, cols), 0)
    j = lax.broadcasted_iota(jnp.int32, (rows, cols), 1)
    if axis == 0:
        return (j // 2 == i).astype(jnp.float32)
    return (i // 2 + shift == j).astype(jnp.float32)


def mm(a, b):
    return jnp.dot(a, b, precision=HIGHEST, preferred_element_type=jnp.float32)


def weight_log(pos, level, n):
    taps = taps_of(level)
    total = jnp.zeros(pos.shape, jnp.float32)
    for d in range(-BAND, BAND + 1):
        inside = (pos + d >= 0) & (pos + d < n)
        total = total + jnp.where(inside, taps[abs(d)], 0.0)
    return jnp.log2(total)


ROUNDS = [
    "g0", "g1", "s2a", "x0", "l0a", "l0b", "l0c", "x1", "l1p", "l1a", "l1b", "l1c",
    "l2p", "l2own", "l2up", "l2down", "fb",
]


FAR_FIRST = sorted(
    [(x, y, z, c) for x in range(4) for y in range(4) for z in range(2) for c in range(2)][1:],
    key=lambda d: -(min(d[0], 4 - d[0]) + min(d[1], 4 - d[1]) + d[2]),
)


def kernel(src_in, tgt_in, f_into, g_into, *scratch):
    names = [name for name, _ in SCRATCH]
    ref = dict(zip(names, scratch))
    io_sem, send_sem, recv_sem = scratch[-3:]
    src, tgt, f_out, g_out = ref["src"], ref["tgt"], ref["f"], ref["g"]
    read_src = pltpu.make_async_copy(src_in, src, io_sem.at[0])
    read_tgt = pltpu.make_async_copy(tgt_in, tgt, io_sem.at[1])
    read_src.start()
    read_tgt.start()
    px = lax.axis_index("px")
    py = lax.axis_index("py")
    zh = py // 2
    core = py % 2
    g = 2 * px + core
    z = 2 * zh + px // 16
    own = 16 * core + px % 16

    barrier = pltpu.get_barrier_semaphore()

    def in_group(q):
        return (q // 2, 2 * zh + q % 2)

    def greet(x, y):
        pl.semaphore_signal(barrier, inc=1, device_id=(x, y), device_id_type=MESH)

    for o in range(1, 32):
        greet((px + o) % 32, own // 4)
    for o in range(1, 8):
        greet(own, (py + o) % 8)

    @pl.when(own // 4 != py)
    def _():
        greet(px, own // 4)

    @pl.when(own != px)
    def _():
        greet(own, py)

    near = [
        [(px % 4 + d) % 4 for d in range(4)],
        [(px // 4 % 4 + d) % 4 for d in range(4)],
        [(px // 16 + d) % 2 for d in range(2)],
        [(core + d) % 2 for d in range(2)],
    ]
    leaving = []

    def exchange(name, n, me, device, src_at, dst_at, most):
        k = ROUNDS.index(name)

        def to(q):
            pltpu.make_async_remote_copy(
                src_ref=src_at(q),
                dst_ref=dst_at(me),
                send_sem=send_sem.at[k],
                recv_sem=recv_sem.at[k],
                device_id=device(q),
                device_id_type=MESH,
            ).start()

        def one(o, carry):
            to((me + o) % n)
            return carry

        if device is plane:
            for dx, dy, dz, dc in FAR_FIRST:
                if dz == 0:
                    to(16 * near[3][dc] + 4 * near[1][dy] + near[0][dx])
        elif n == 64:
            for dx, dy, dz, dc in FAR_FIRST:
                to(2 * (16 * near[2][dz] + 4 * near[1][dy] + near[0][dx]) + near[3][dc])
        else:
            lax.fori_loop(1, n, one, 0)
        pltpu.make_async_copy(src_at(me), dst_at(me), recv_sem.at[k]).start()
        leaving.append((name, most))

    def arrived(name, whole):
        k = ROUNDS.index(name)
        pltpu.make_async_copy(whole, whole, recv_sem.at[k]).wait()

    def sent(name, part):
        k = ROUNDS.index(name)
        pltpu.make_async_copy(part, part, send_sem.at[k]).wait()

    def column(q):
        return (px, q)

    def plane(q):
        return (16 * (px // 16) + q % 16, 2 * zh + q // 16)

    def pencil(q):
        return (q, py)

    for name, n in (("m0", 64), ("t0", 64), ("r0", 64), ("m1", 128), ("t1", 128), ("r1", 128), ("c1", 64), ("u2", 128),
                    ("l2pr", 128), ("m2", 256), ("k2", 256)):
        border(ref[name], n)

    read_src.wait()
    read_tgt.wait()
    es, ms = [], []
    for arr in (src, tgt):
        for d in range(4):
            a = arr[2 * d] * LOG2E
            b = arr[2 * d + 1] * LOG2E
            m = pair_max(pair_max(jnp.maximum(a, b), 0), 1)
            es.append(jnp.exp2(a - m) + jnp.exp2(b - m))
            ms.append(m)
    fine = mm(jnp.concatenate(es + ms, axis=0), halving(256, 128, 1))
    rows = halving(128, 256, 0)
    r1 = mm(rows, fine[256:]) * 0.25 + jnp.log2(mm(rows, fine[:256])) - 3.0
    s1 = ref["g1s"]
    for i in range(8):
        s1[i // 4, i % 4] = r1[16 * i : 16 * i + 16]
    es, ms = [], []
    for d in range(2):
        for arr in range(2):
            o = (arr * 4 + 2 * d) * 16
            a, b = r1[o : o + 16], r1[o + 16 : o + 32]
            m = pair_max(pair_max(jnp.maximum(a, b), 0), 1)
            es.append(jnp.exp2(a - m) + jnp.exp2(b - m))
            ms.append(m)

    def packed(v):
        low = mm(jnp.concatenate(v[:2], axis=0), halving(128, 128, 1))
        high = mm(jnp.concatenate(v[2:], axis=0), halving(128, 128, 1, 64))
        return mm(halving(16, 32, 0), low + high)

    r0 = packed(ms) * 0.25 + jnp.log2(packed(es)) - 3.0
    s0 = ref["g0s"]
    s0[0] = r0[:8]
    s0[1] = r0[8:]

    own_source = (own // 4 == py).astype(jnp.int32)
    own_target = (own == px).astype(jnp.int32)
    pl.semaphore_wait(barrier, 40 - own_source - own_target)

    r_g1, r_s2a = ref["g1r"], ref["s2ar"]
    x0r, a0, b0 = ref["x0r"], ref["a0"], ref["b0"]
    k_x0, k_g0 = ROUNDS.index("x0"), ROUNDS.index("g0")

    def first_send(k, part, place, x, y):
        pltpu.make_async_remote_copy(
            src_ref=part,
            dst_ref=place,
            send_sem=send_sem.at[k],
            recv_sem=recv_sem.at[k],
            device_id=(x, y),
            device_id_type=MESH,
        ).start()

    def first_own(k, part, place):
        pltpu.make_async_copy(part, place, recv_sem.at[k]).start()

    for o in (4, 3, 5, 2, 6, 1, 7, 0):
        to_z = (z + o) % 8
        for r in range(4):
            p = 4 * py + r
            x, y = 16 * (to_z % 2) + p % 16, 2 * (to_z // 2) + p // 16
            part, place = s0.at[0, pl.ds(2 * r, 2)], x0r.at[pl.ds(2 * px, 2)]
            if o:
                first_send(k_x0, part, place, x, y)
            else:
                pl.when(p != own)(functools.partial(first_send, k_x0, part, place, x, y))
                pl.when(p == own)(functools.partial(first_own, k_x0, part, place))
    for o in (4, 3, 5, 2, 6, 1, 7, 0):
        to_z = (z + o) % 8
        x, y = 16 * (to_z % 2) + px % 16, 2 * (to_z // 2) + px // 16
        part, place = s0.at[1], b0.at[pl.ds(8 * py, 8)]
        if o:
            first_send(k_g0, part, place, x, y)
        else:
            pl.when(own != px)(functools.partial(first_send, k_g0, part, place, x, y))
            pl.when(own == px)(functools.partial(first_own, k_g0, part, place))

    m0, t0, q0, w0 = ref["m0"], ref["t0"], ref["r0"], ref["w0"]

    lanes0 = lax.broadcasted_iota(jnp.int32, (64, 128), 1)
    zero0 = (
        weight_log(lax.broadcasted_iota(jnp.int32, (64, 128), 0), 0, 64)
        + weight_log(lanes0 % 64, 0, 64)
        + weight_log(2 * own + lanes0 // 64, 0, 64)
    )

    def turn0(v):
        t = jnp.concatenate([v, v], axis=0).T
        return jnp.where(lane_lo((64, 128)), t[:64], t[64:])

    def scatter0(r, store):
        a, b = mix(r[pl.ds(0, 32, stride=2), :], r[pl.ds(1, 32, stride=2), :])
        store(0, a)
        store(1, b)

    def swap0(name, s, r):
        exchange(
            name, 32, own, plane,
            lambda q: s.at[pl.ds(2 * q, 2)],
            lambda q: r.at[pl.ds(2 * q, 2)],
            r.at[pl.ds(0, 62)],
        )

    arrived("x0", x0r)

    def put_a0(k, v):
        a0[pl.ds(k, 32, stride=2), :] = v

    scatter0(x0r, put_a0)
    m0[0, pl.ds(BAND, 64), :] = a0[...] - zero0

    def transform0(name, other, background):
        s, r = ref[name + "s"], ref[name + "r"]

        def put_w(p, c, v):
            w0[every2(c), :] = v

        soft_rows(m0, 1, 64, 0, put_w)
        t0[0, pl.ds(BAND, 64), :] = turn0(w0[...])
        soft_rows(t0, 1, 64, 0, put_w)
        s[...] = turn0(w0[...])
        swap0(name, s, r)
        background()
        arrived(name, r)

        def put_r(k, v):
            q0[0, pl.ds(BAND + k, 32, stride=2), :] = v

        scatter0(r, put_r)

        def finish(p, c, v):
            m0[0, every2(BAND + c), :] = other[every2(c), :] - v

        soft_rows(q0, 1, 64, 0, finish)

    m1, t1, q1, w1 = ref["m1"], ref["t1"], ref["r1"], ref["w1"]
    a1, b1 = ref["a1"], ref["b1"]

    def swap1(name, s, r):
        exchange(
            name, 64, g, in_group,
            lambda q: s.at[:, pl.ds(2 * q, 2)],
            lambda q: r.at[:, pl.ds(2 * q, 2)],
            r.at[:, pl.ds(0, 126)],
        )

    def scatter1(r, store):
        for a in range(2):
            for b in range(2):
                store(b, a, r[a, every2(b, 64), :])

    def source1_out():
        arrived("g1", r_g1)
        for i in range(8):
            for a in range(2):
                ref["x1s"][a, 16 * i : 16 * i + 16, :] = r_g1[i, 0, a]
                b1[a, 16 * i : 16 * i + 16, :] = r_g1[i, 1, a]
        swap1("x1", ref["x1s"], ref["x1r"])

    def source2_out():
        exchange(
            "s2a", 32, px, pencil,
            lambda q: src.at[:, q],
            lambda q: r_s2a.at[pl.ds(8 * q, 8)],
            r_s2a.at[pl.ds(0, 248)],
        )

    def source1_in():
        arrived("x1", ref["x1r"])

        def put(b, a, v):
            a1[b, pl.ds(a, 64, stride=2), :] = v

        scatter1(ref["x1r"], put)

    def first_background():
        exchange(
            "g1", 8, py, column,
            lambda q: s1.at[:, pl.ds(2 * (q % 2), 2)],
            lambda q: r_g1.at[q],
            r_g1.at[pl.ds(0, 7)],
        )
        source2_out()
        arrived("g0", b0)

    transform0("l0a", b0, first_background)
    transform0("l0b", a0, source1_out)
    transform0("l0c", b0, lambda: None)

    g0 = m0[0, pl.ds(BAND, 64), :] * 2.0
    mine = jnp.where(px < 16, g0, half(g0))
    c1, u1 = ref["c1"], ref["u1"]
    c1[0, pl.ds(BAND, 64), :] = mine

    def put_u(p, c, s, v):
        u1[pl.ds(2 * c + s, 32, stride=2), :] = v

    soft_rows_copied(c1, 1, 0, 64, 1, put_u)
    c1[0, pl.ds(BAND, 64), :] = u1[...].T[:64]
    soft_rows_copied(c1, 1, 0, 64, 1, put_u)
    l1ps, l1pr = ref["l1ps"], ref["l1pr"]
    l1ps[...] = u1[...].T
    coarse = 2 * own + px // 16
    exchange(
        "l1p", 64, g, in_group,
        lambda q: l1ps.at[pl.ds(2 * q, 2)],
        lambda q: l1pr.at[pl.ds(2 * coarse, 2)],
        l1pr.at[pl.ds(0, 126)],
    )
    source1_in()
    arrived("l1p", l1pr)

    def finish_l1p(b):
        def put(p, c, s, v):
            m1[b, pl.ds(BAND + 2 * c + s, 32, stride=2), :] = a1[b, pl.ds(2 * c + s, 32, stride=2), :] - v

        return put

    for b in range(2):
        c1[0, pl.ds(BAND, 64), :] = l1pr[pl.ds(b, 64, stride=2), :]
        soft_rows_copied(c1, 1, 0, 64, 1, finish_l1p(b))

    def transform1(name, other, background, times=1.0):
        s, r = ref[name + "s"], ref[name + "r"]

        def put_w(p, c, v):
            w1[p, every2(c), :] = v

        soft_rows(m1, 2, 128, 1, put_w)
        for p in range(2):
            t1[p, pl.ds(BAND, 128), :] = w1[p].T
        soft_rows(t1, 2, 128, 1, put_w)
        for p in range(2):
            s[p] = w1[p].T
        swap1(name, s, r)
        background()
        arrived(name, r)

        def put_r(b, a, v):
            q1[b, pl.ds(BAND + a, 64, stride=2), :] = v

        scatter1(r, put_r)

        def finish(p, c, v):
            m1[p, every2(BAND + c), :] = (other[p, every2(c), :] - v) * times

        soft_rows(q1, 2, 128, 1, finish)

    a2 = ref["a2"]

    def source2_in():
        arrived("s2a", r_s2a)
        for h in range(2):
            a2[h] = r_s2a[:, 128 * h : 128 * h + 128] * LOG2E

    transform1("l1a", b1, source2_in)
    transform1("l1b", a1, lambda: None)
    transform1("l1c", b1, lambda: None, 2.0)

    w2, u2, l2ps, l2pr = ref["w2"], ref["u2"], ref["l2ps"], ref["l2pr"]

    def put_w2(p, c, s, v):
        w2[pl.ds(64 * p + 2 * c + s, 32, stride=2), :] = v

    soft_rows_copied(m1, 2, pl.multiple_of(32 * zh, 32), 32, 2, put_w2)
    u2[0, pl.ds(BAND, 128), :] = w2[...].T
    w3 = ref["w3"]

    def put_w3(p, c, s, v):
        w3[0, pl.ds(2 * c + s, 32, stride=2), :] = v

    soft_rows_copied(u2, 1, 0, 128, 2, put_w3)
    for h in range(2):
        t = w3[0, 128 * h : 128 * h + 128, :].T
        for a in range(2):
            l2ps[h, pl.ds(a, 64, stride=2), :] = t[64 * a : 64 * a + 64]
    exchange(
        "l2p", 64, g, in_group,
        lambda q: l2ps.at[:, pl.ds(2 * (32 * (q % 2) + q // 2), 2)],
        lambda q: l2pr.at[:, pl.ds(BAND + 2 * q, 2)],
        l2pr.at[:, pl.ds(0, 126)],
    )
    arrived("l2p", l2pr.at[:, pl.ds(BAND, 128)])
    m2, k2, fbr = ref["m2"], ref["k2"], ref["fbr"]

    def put_m2(p, c, s, v):
        m2[p, pl.ds(BAND + 2 * c + s, 32, stride=2), :] = a2[p, pl.ds(2 * c + s, 32, stride=2), :] - v

    soft_rows_copied(l2pr, 2, 0, 128, 2, put_m2)
    exchange(
        "fb", 32, px, pencil,
        lambda q: m2.at[:, pl.ds(BAND + 8 * q, 8)],
        lambda q: fbr.at[:, pl.ds(8 * q, 8)],
        fbr.at[:, pl.ds(0, 248)],
    )

    def put_w(p, c, v):
        w3[p, every2(c), :] = v

    def turn2(store):
        for i in range(2):
            for j in range(2):
                store(i, j, w3[j, 128 * i : 128 * i + 128, :].T)

    def put_k2(i, j, v):
        k2[i, pl.ds(BAND + 128 * j, 128), :] = v

    soft_rows(m2, 2, 256, 2, put_w)
    turn2(put_k2)
    l2s, l2r = ref["l2s"], ref["l2r"]

    low = px < 16
    beside = jnp.where(low, py - 1, py + 1)
    has_beside = (beside >= 0) & (beside < 8)
    k_own = ROUNDS.index("l2own")
    k_beside = jnp.where(low, ROUNDS.index("l2down"), ROUNDS.index("l2up"))
    place = jnp.where(low, 48 + px, px - 16)

    def last_send(k, q, row, y):
        pltpu.make_async_remote_copy(
            src_ref=l2s.at[:, pl.ds(8 * q, 8)],
            dst_ref=l2r.at[row],
            send_sem=send_sem.at[k],
            recv_sem=recv_sem.at[k],
            device_id=(q, y),
            device_id_type=MESH,
        ).start()

    def last_own():
        pltpu.make_async_copy(l2s.at[:, pl.ds(8 * px, 8)], l2r.at[BAND + px], recv_sem.at[k_own]).start()

    for i in range(2):

        def put_half(p, c, v, i=i):
            w3[i, every2(c), :] = v

        soft_rows(k2.at[pl.ds(i, 1)], 1, 256, 2, put_half)
        for h in range(2):
            l2s[h, 128 * i : 128 * i + 128, :] = w3[i, 128 * h : 128 * h + 128, :].T
        to = [16 * i + 4 * near[1][dy] + near[0][dx] for dx, dy, dz, dc in FAR_FIRST if dz == dc == 0]
        to = to + [16 * i + px % 16]

        def beside_half(to=to):
            for q in to:
                last_send(k_beside, q, place, beside)

        pl.when(has_beside)(beside_half)
        for q in to[:-1]:
            last_send(k_own, q, BAND + px, py)
        pl.when(px // 16 != i)(functools.partial(last_send, k_own, to[-1], BAND + px, py))
    last_own()
    leaving.append(("l2own", l2r.at[pl.ds(0, 31)]))

    arrived("fb", fbr)
    for d in range(8):
        for h in range(2):
            f_out[d, :, 128 * h : 128 * h + 128] = fbr[h, pl.ds(d, 32, stride=8), :]
    write_f = pltpu.make_async_copy(f_out, f_into, io_sem.at[2])
    write_f.start()

    arrived("l2own", l2r.at[pl.ds(BAND, 32)])
    edge = jnp.full((BAND, 2, 8, 128), NEG, jnp.float32)

    @pl.when(py > 0)
    def _():
        arrived("l2up", l2r.at[pl.ds(0, BAND)])

    @pl.when(py == 0)
    def _():
        l2r[pl.ds(0, BAND)] = edge

    @pl.when(py < 7)
    def _():
        arrived("l2down", l2r.at[pl.ds(48, BAND)])

    @pl.when(py == 7)
    def _():
        l2r[pl.ds(48, BAND)] = edge

    def put_rows(r, h, v):
        w3[h, pl.ds(r, 8, stride=32), :] = v

    soft_major(l2r, 32, 2, put_rows)
    for h in range(2):
        cols = slice(128 * h, 128 * h + 128)
        for d in range(8):
            g_out[d, :, cols] = w3[h, 32 * d : 32 * d + 32, :]
    write_g = pltpu.make_async_copy(g_out, g_into, io_sem.at[3])
    write_g.start()

    @pl.when(has_beside & low)
    def _():
        sent("l2down", l2r.at[pl.ds(0, 32)])

    @pl.when(has_beside & jnp.logical_not(low))
    def _():
        sent("l2up", l2r.at[pl.ds(0, 32)])

    write_f.wait()
    write_g.wait()
    for name, part in leaving:
        sent(name, part)
    sent("x0", x0r.at[pl.ds(0, 62)])
    sent("g0", b0.at[pl.ds(0, 56)])
    pl.when(own // 4 != py)(lambda: sent("x0", x0r.at[pl.ds(0, 2)]))
    pl.when(own != px)(lambda: sent("g0", b0.at[pl.ds(0, 8)]))


SCRATCH = [
    ("src", (8, 32, 256)), ("tgt", (8, 32, 256)), ("f", (8, 32, 256)), ("g", (8, 32, 256)),
    ("g0s", (2, 8, 128)),
    ("g1s", (2, 4, 16, 128)), ("g1r", (8, 2, 2, 16, 128)),
    ("s2ar", (256, 256)),
    ("x0r", (64, 128)),
    ("l0as", (64, 128)), ("l0ar", (64, 128)), ("l0bs", (64, 128)), ("l0br", (64, 128)),
    ("l0cs", (64, 128)), ("l0cr", (64, 128)),
    ("x1s", (2, 128, 128)), ("x1r", (2, 128, 128)),
    ("l1ps", (128, 128)), ("l1pr", (128, 128)),
    ("l1as", (2, 128, 128)), ("l1ar", (2, 128, 128)), ("l1bs", (2, 128, 128)), ("l1br", (2, 128, 128)),
    ("l1cs", (2, 128, 128)), ("l1cr", (2, 128, 128)),
    ("l2ps", (2, 128, 128)), ("l2pr", (2, 160, 128)),
    ("l2s", (2, 256, 128)), ("l2r", (64, 2, 8, 128)),
    ("fbr", (2, 256, 128)),
    ("m0", (1, 96, 128)), ("t0", (1, 96, 128)), ("r0", (1, 96, 128)), ("w0", (64, 128)),
    ("a0", (64, 128)), ("b0", (64, 128)),
    ("m1", (2, 160, 128)), ("t1", (2, 160, 128)), ("r1", (2, 160, 128)), ("w1", (2, 128, 128)),
    ("a1", (2, 128, 128)), ("b1", (2, 128, 128)),
    ("c1", (1, 96, 128)), ("u1", (128, 128)),
    ("u2", (1, 160, 128)), ("w2", (128, 128)), ("a2", (2, 256, 128)),
    ("m2", (2, 288, 128)), ("k2", (2, 288, 128)), ("w3", (2, 256, 128)),
]


def per_device(log_source, log_target):
    shape = jax.ShapeDtypeStruct((8, 32, 256), jnp.float32)
    anywhere = pl.BlockSpec(memory_space=pl.ANY)
    scaled_f, pulled = pl.pallas_call(
        kernel,
        out_shape=(shape, shape),
        in_specs=[anywhere, anywhere],
        out_specs=(anywhere, anywhere),
        scratch_shapes=[pltpu.VMEM(s, jnp.float32) for _, s in SCRATCH]
        + [pltpu.SemaphoreType.DMA((4,)), pltpu.SemaphoreType.DMA((len(ROUNDS),)), pltpu.SemaphoreType.DMA((len(ROUNDS),))],
        compiler_params=pltpu.CompilerParams(collective_id=0, has_side_effects=True),
        name="sinkhorn",
    )(log_source, log_target)
    return 0.05 * LN2 * scaled_f, 0.05 * log_target - 0.05 * LN2 * pulled


def solution(mesh):
    return jax.shard_map(
        per_device,
        mesh=mesh,
        in_specs=(P("px", "py", None), P("px", "py", None)),
        out_specs=(P("px", "py", None), P("px", "py", None)),
        check_vma=False,
    )
```

```python
import functools
import math

import jax
import jax.numpy as jnp
from jax import lax
from jax.experimental import pallas as pl
from jax.experimental.pallas import tpu as pltpu
from jax.sharding import PartitionSpec as P

LEVELS = 3
BAND = 16
NEG = -1e30
LOG2E = 1.4426950408889634
LN2 = 0.6931471805599453
MESH = pl.DeviceIdType.MESH
HIGHEST = lax.Precision.HIGHEST


def taps_of(level):
    inverse_width = 2.0 ** (LEVELS - 1 - level) / 18.0
    return [math.exp(-float(d * d) * inverse_width) for d in range(BAND + 1)]


def coarse_taps(level):
    taps = taps_of(level)
    weights = []
    for s in range(2):
        weights.append(
            [
                sum(taps[abs(2 * D + u - s)] for u in range(2) if abs(2 * D + u - s) <= BAND)
                for D in range(-BAND // 2, BAND // 2 + 1)
            ]
        )
    return weights


def lane_lo(shape):
    return lax.broadcasted_iota(jnp.int32, shape, 1) < 64


def half(v):
    return pltpu.roll(v, 64, 1)


def mix(a, b):
    lo = lane_lo(a.shape)
    return jnp.where(lo, a, half(b)), jnp.where(lo, half(a), b)


def tree(op, xs):
    xs = list(xs)
    while len(xs) > 1:
        xs = [op(xs[i], xs[i + 1]) if i + 1 < len(xs) else xs[i] for i in range(0, len(xs), 2)]
    return xs[0]


def soft_pair(tap, taps):
    shared = tree(jnp.maximum, [tap(t) for t in range(1, 2 * BAND + 1)])
    e = {t: jnp.exp2(tap(t) - shared) for t in range(1, 2 * BAND + 1)}
    outs = []
    for k in range(2):
        mid = BAND + k
        parts = [taps[0] * e[mid]]
        parts += [taps[d] * (e[mid - d] + e[mid + d]) for d in range(1, BAND)]
        parts += [taps[BAND] * e[1 if k else 2 * BAND]]
        accs = [tree(jnp.add, parts[i::4]) for i in range(4)]
        total = (accs[0] + accs[1]) + (accs[2] + accs[3])
        last = tap((2 * BAND + 1) * k)
        m = jnp.maximum(shared, last)
        total = total * jnp.exp2(shared - m) + taps[BAND] * jnp.exp2(last - m)
        outs.append(m + jnp.log2(total))
    return outs


def soft_rows(pad, planes, n, level, store, units=8):
    taps = taps_of(level)
    units = min(units, n // 16)
    size = 16 * units
    per = n // size

    def body(it, carry):
        p = it // per
        base = pl.multiple_of((it % per) * size, size)
        for u in range(units):
            c = base + 16 * u
            outs = soft_pair(lambda t, c=c: pad[p, pl.ds(c + t, 8, stride=2), :], taps)
            for k in range(2):
                store(p, c + k, outs[k])
        return carry

    lax.fori_loop(0, planes * per, body, 0)


def every2(start, count=8):
    return pl.ds(start, count, stride=2)


def soft_rows_copied(pad, planes, first, n, level, store, chunk=32):
    weights = coarse_taps(level)
    per = n // chunk

    def body(it, carry):
        p = it // per
        c = pl.multiple_of((it % per) * chunk, chunk)

        def tap(t):
            return pad[p, pl.ds(first + c + BAND // 2 + t, chunk), :]

        m = tree(jnp.maximum, [tap(t) for t in range(BAND + 1)])
        es = [jnp.exp2(tap(t) - m) for t in range(BAND + 1)]
        for s in range(2):
            total = tree(jnp.add, [weights[s][t] * es[t] for t in range(BAND + 1)])
            store(p, c, s, m + jnp.log2(total))
        return carry

    lax.fori_loop(0, planes * per, body, 0)


def soft_major(buf, n, level, store, units=4):
    taps = taps_of(level)
    size = 2 * units
    per = n // size

    def body(it, carry):
        h = it // per
        base = (it % per) * size
        for u in range(units):
            c = base + 2 * u
            outs = soft_pair(lambda t, c=c: buf[c + t, h], taps)
            for k in range(2):
                store(c + k, h, outs[k])
        return carry

    lax.fori_loop(0, 2 * per, body, 0)


def border(pad, n):
    planes, _, lanes = pad.shape
    for p in range(planes):
        pad[p, pl.ds(0, BAND), :] = jnp.full((BAND, lanes), NEG, jnp.float32)
        pad[p, pl.ds(BAND + n, BAND), :] = jnp.full((BAND, lanes), NEG, jnp.float32)


def pair_max(v, axis):
    n = v.shape[axis]
    even = lax.broadcasted_iota(jnp.int32, v.shape, axis) % 2 == 0
    other = jnp.where(even, pltpu.roll(v, n - 1, axis), pltpu.roll(v, 1, axis))
    return jnp.maximum(v, other)


def halving(rows, cols, axis, shift=0):
    i = lax.broadcasted_iota(jnp.int32, (rows, cols), 0)
    j = lax.broadcasted_iota(jnp.int32, (rows, cols), 1)
    if axis == 0:
        return (j // 2 == i).astype(jnp.float32)
    return (i // 2 + shift == j).astype(jnp.float32)


def mm(a, b):
    return jnp.dot(a, b, precision=HIGHEST, preferred_element_type=jnp.float32)


def weight_log(pos, level, n):
    taps = taps_of(level)
    total = jnp.zeros(pos.shape, jnp.float32)
    for d in range(-BAND, BAND + 1):
        inside = (pos + d >= 0) & (pos + d < n)
        total = total + jnp.where(inside, taps[abs(d)], 0.0)
    return jnp.log2(total)


ROUNDS = [
    "g0", "g1", "s2a", "x0", "l0a", "l0b", "l0c", "x1", "l1p", "l1a", "l1b", "l1c",
    "l2p", "l2own", "l2up", "l2down", "fb",
]


FAR_FIRST = sorted(
    [(x, y, z, c) for x in range(4) for y in range(4) for z in range(2) for c in range(2)][1:],
    key=lambda d: -(min(d[0], 4 - d[0]) + min(d[1], 4 - d[1]) + d[2]),
)


def kernel(src_in, tgt_in, f_into, g_into, *scratch):
    names = [name for name, _ in SCRATCH]
    ref = dict(zip(names, scratch))
    io_sem, send_sem, recv_sem = scratch[-3:]
    src, tgt, f_out, g_out = ref["src"], ref["tgt"], ref["f"], ref["g"]
    read_src = pltpu.make_async_copy(src_in, src, io_sem.at[0])
    read_tgt = pltpu.make_async_copy(tgt_in, tgt, io_sem.at[1])
    read_src.start()
    read_tgt.start()
    px = lax.axis_index("px")
    py = lax.axis_index("py")
    zh = py // 2
    core = py % 2
    g = 2 * px + core
    z = 2 * zh + px // 16
    own = 16 * core + px % 16

    barrier = pltpu.get_barrier_semaphore()

    def in_group(q):
        return (q // 2, 2 * zh + q % 2)

    def greet(x, y):
        pl.semaphore_signal(barrier, inc=1, device_id=(x, y), device_id_type=MESH)

    for o in range(1, 32):
        greet((px + o) % 32, own // 4)
    for o in range(1, 8):
        greet(own, (py + o) % 8)

    @pl.when(own // 4 != py)
    def _():
        greet(px, own // 4)

    @pl.when(own != px)
    def _():
        greet(own, py)

    near = [
        [(px % 4 + d) % 4 for d in range(4)],
        [(px // 4 % 4 + d) % 4 for d in range(4)],
        [(px // 16 + d) % 2 for d in range(2)],
        [(core + d) % 2 for d in range(2)],
    ]
    leaving = []

    def exchange(name, n, me, device, src_at, dst_at, most):
        k = ROUNDS.index(name)

        def to(q):
            pltpu.make_async_remote_copy(
                src_ref=src_at(q),
                dst_ref=dst_at(me),
                send_sem=send_sem.at[k],
                recv_sem=recv_sem.at[k],
                device_id=device(q),
                device_id_type=MESH,
            ).start()

        def one(o, carry):
            to((me + o) % n)
            return carry

        if device is plane:
            for dx, dy, dz, dc in FAR_FIRST:
                if dz == 0:
                    to(16 * near[3][dc] + 4 * near[1][dy] + near[0][dx])
        elif device is pencil:
            for dx, dy, dz, dc in FAR_FIRST:
                if dc == 0:
                    to(16 * near[2][dz] + 4 * near[1][dy] + near[0][dx])
        elif n == 64:
            for dx, dy, dz, dc in FAR_FIRST:
                to(2 * (16 * near[2][dz] + 4 * near[1][dy] + near[0][dx]) + near[3][dc])
        else:
            lax.fori_loop(1, n, one, 0)
        pltpu.make_async_copy(src_at(me), dst_at(me), recv_sem.at[k]).start()
        leaving.append((name, most))

    def arrived(name, whole):
        k = ROUNDS.index(name)
        pltpu.make_async_copy(whole, whole, recv_sem.at[k]).wait()

    def sent(name, part):
        k = ROUNDS.index(name)
        pltpu.make_async_copy(part, part, send_sem.at[k]).wait()

    def column(q):
        return (px, q)

    def plane(q):
        return (16 * (px // 16) + q % 16, 2 * zh + q // 16)

    def pencil(q):
        return (q, py)

    for name, n in (("m0", 64), ("t0", 64), ("r0", 64), ("m1", 128), ("t1", 128), ("r1", 128), ("c1", 64), ("u2", 128),
                    ("l2pr", 128), ("m2", 256), ("k2", 256)):
        border(ref[name], n)

    read_src.wait()
    read_tgt.wait()
    es, ms = [], []
    for arr in (src, tgt):
        for d in range(4):
            a = arr[2 * d] * LOG2E
            b = arr[2 * d + 1] * LOG2E
            m = pair_max(pair_max(jnp.maximum(a, b), 0), 1)
            es.append(jnp.exp2(a - m) + jnp.exp2(b - m))
            ms.append(m)
    fine = mm(jnp.concatenate(es + ms, axis=0), halving(256, 128, 1))
    rows = halving(128, 256, 0)
    r1 = mm(rows, fine[256:]) * 0.25 + jnp.log2(mm(rows, fine[:256])) - 3.0
    s1 = ref["g1s"]
    for i in range(8):
        s1[i // 4, i % 4] = r1[16 * i : 16 * i + 16]
    es, ms = [], []
    for d in range(2):
        for arr in range(2):
            o = (arr * 4 + 2 * d) * 16
            a, b = r1[o : o + 16], r1[o + 16 : o + 32]
            m = pair_max(pair_max(jnp.maximum(a, b), 0), 1)
            es.append(jnp.exp2(a - m) + jnp.exp2(b - m))
            ms.append(m)

    def packed(v):
        low = mm(jnp.concatenate(v[:2], axis=0), halving(128, 128, 1))
        high = mm(jnp.concatenate(v[2:], axis=0), halving(128, 128, 1, 64))
        return mm(halving(16, 32, 0), low + high)

    r0 = packed(ms) * 0.25 + jnp.log2(packed(es)) - 3.0
    s0 = ref["g0s"]
    s0[0] = r0[:8]
    s0[1] = r0[8:]

    own_source = (own // 4 == py).astype(jnp.int32)
    own_target = (own == px).astype(jnp.int32)
    pl.semaphore_wait(barrier, 40 - own_source - own_target)

    r_g1, r_s2a = ref["g1r"], ref["s2ar"]
    x0r, a0, b0 = ref["x0r"], ref["a0"], ref["b0"]
    k_x0, k_g0 = ROUNDS.index("x0"), ROUNDS.index("g0")

    def first_send(k, part, place, x, y):
        pltpu.make_async_remote_copy(
            src_ref=part,
            dst_ref=place,
            send_sem=send_sem.at[k],
            recv_sem=recv_sem.at[k],
            device_id=(x, y),
            device_id_type=MESH,
        ).start()

    def first_own(k, part, place):
        pltpu.make_async_copy(part, place, recv_sem.at[k]).start()

    for o in (4, 3, 5, 2, 6, 1, 7, 0):
        to_z = (z + o) % 8
        for r in range(4):
            p = 4 * py + r
            x, y = 16 * (to_z % 2) + p % 16, 2 * (to_z // 2) + p // 16
            part, place = s0.at[0, pl.ds(2 * r, 2)], x0r.at[pl.ds(2 * px, 2)]
            if o:
                first_send(k_x0, part, place, x, y)
            else:
                pl.when(p != own)(functools.partial(first_send, k_x0, part, place, x, y))
                pl.when(p == own)(functools.partial(first_own, k_x0, part, place))
    for o in (4, 3, 5, 2, 6, 1, 7, 0):
        to_z = (z + o) % 8
        x, y = 16 * (to_z % 2) + px % 16, 2 * (to_z // 2) + px // 16
        part, place = s0.at[1], b0.at[pl.ds(8 * py, 8)]
        if o:
            first_send(k_g0, part, place, x, y)
        else:
            pl.when(own != px)(functools.partial(first_send, k_g0, part, place, x, y))
            pl.when(own == px)(functools.partial(first_own, k_g0, part, place))

    m0, t0, q0, w0 = ref["m0"], ref["t0"], ref["r0"], ref["w0"]

    lanes0 = lax.broadcasted_iota(jnp.int32, (64, 128), 1)
    zero0 = (
        weight_log(lax.broadcasted_iota(jnp.int32, (64, 128), 0), 0, 64)
        + weight_log(lanes0 % 64, 0, 64)
        + weight_log(2 * own + lanes0 // 64, 0, 64)
    )

    def turn0(v):
        t = jnp.concatenate([v, v], axis=0).T
        return jnp.where(lane_lo((64, 128)), t[:64], t[64:])

    def scatter0(r, store):
        a, b = mix(r[pl.ds(0, 32, stride=2), :], r[pl.ds(1, 32, stride=2), :])
        store(0, a)
        store(1, b)

    def swap0(name, s, r):
        exchange(
            name, 32, own, plane,
            lambda q: s.at[pl.ds(2 * q, 2)],
            lambda q: r.at[pl.ds(2 * q, 2)],
            r.at[pl.ds(0, 62)],
        )

    arrived("x0", x0r)

    def put_a0(k, v):
        a0[pl.ds(k, 32, stride=2), :] = v

    scatter0(x0r, put_a0)
    m0[0, pl.ds(BAND, 64), :] = a0[...] - zero0

    def transform0(name, other, background):
        s, r = ref[name + "s"], ref[name + "r"]

        def put_w(p, c, v):
            w0[every2(c), :] = v

        soft_rows(m0, 1, 64, 0, put_w)
        t0[0, pl.ds(BAND, 64), :] = turn0(w0[...])
        soft_rows(t0, 1, 64, 0, put_w)
        s[...] = turn0(w0[...])
        swap0(name, s, r)
        background()
        arrived(name, r)

        def put_r(k, v):
            q0[0, pl.ds(BAND + k, 32, stride=2), :] = v

        scatter0(r, put_r)

        def finish(p, c, v):
            m0[0, every2(BAND + c), :] = other[every2(c), :] - v

        soft_rows(q0, 1, 64, 0, finish)

    m1, t1, q1, w1 = ref["m1"], ref["t1"], ref["r1"], ref["w1"]
    a1, b1 = ref["a1"], ref["b1"]

    def swap1(name, s, r):
        exchange(
            name, 64, g, in_group,
            lambda q: s.at[:, pl.ds(2 * q, 2)],
            lambda q: r.at[:, pl.ds(2 * q, 2)],
            r.at[:, pl.ds(0, 126)],
        )

    def scatter1(r, store):
        for a in range(2):
            for b in range(2):
                store(b, a, r[a, every2(b, 64), :])

    def source1_out():
        arrived("g1", r_g1)
        for i in range(8):
            for a in range(2):
                ref["x1s"][a, 16 * i : 16 * i + 16, :] = r_g1[i, 0, a]
                b1[a, 16 * i : 16 * i + 16, :] = r_g1[i, 1, a]
        swap1("x1", ref["x1s"], ref["x1r"])

    def source2_out():
        exchange(
            "s2a", 32, px, pencil,
            lambda q: src.at[:, q],
            lambda q: r_s2a.at[pl.ds(8 * q, 8)],
            r_s2a.at[pl.ds(0, 248)],
        )

    def source1_in():
        arrived("x1", ref["x1r"])

        def put(b, a, v):
            a1[b, pl.ds(a, 64, stride=2), :] = v

        scatter1(ref["x1r"], put)

    def first_background():
        exchange(
            "g1", 8, py, column,
            lambda q: s1.at[:, pl.ds(2 * (q % 2), 2)],
            lambda q: r_g1.at[q],
            r_g1.at[pl.ds(0, 7)],
        )
        source2_out()
        arrived("g0", b0)

    transform0("l0a", b0, first_background)
    transform0("l0b", a0, source1_out)
    transform0("l0c", b0, lambda: None)

    g0 = m0[0, pl.ds(BAND, 64), :] * 2.0
    mine = jnp.where(px < 16, g0, half(g0))
    c1, u1 = ref["c1"], ref["u1"]
    c1[0, pl.ds(BAND, 64), :] = mine

    def put_u(p, c, s, v):
        u1[pl.ds(2 * c + s, 32, stride=2), :] = v

    soft_rows_copied(c1, 1, 0, 64, 1, put_u)
    c1[0, pl.ds(BAND, 64), :] = u1[...].T[:64]
    soft_rows_copied(c1, 1, 0, 64, 1, put_u)
    l1ps, l1pr = ref["l1ps"], ref["l1pr"]
    l1ps[...] = u1[...].T
    coarse = 2 * own + px // 16
    exchange(
        "l1p", 64, g, in_group,
        lambda q: l1ps.at[pl.ds(2 * q, 2)],
        lambda q: l1pr.at[pl.ds(2 * coarse, 2)],
        l1pr.at[pl.ds(0, 126)],
    )
    source1_in()
    arrived("l1p", l1pr)

    def finish_l1p(b):
        def put(p, c, s, v):
            m1[b, pl.ds(BAND + 2 * c + s, 32, stride=2), :] = a1[b, pl.ds(2 * c + s, 32, stride=2), :] - v

        return put

    for b in range(2):
        c1[0, pl.ds(BAND, 64), :] = l1pr[pl.ds(b, 64, stride=2), :]
        soft_rows_copied(c1, 1, 0, 64, 1, finish_l1p(b))

    def transform1(name, other, background, times=1.0):
        s, r = ref[name + "s"], ref[name + "r"]

        def put_w(p, c, v):
            w1[p, every2(c), :] = v

        soft_rows(m1, 2, 128, 1, put_w)
        for p in range(2):
            t1[p, pl.ds(BAND, 128), :] = w1[p].T
        soft_rows(t1, 2, 128, 1, put_w)
        for p in range(2):
            s[p] = w1[p].T
        swap1(name, s, r)
        background()
        arrived(name, r)

        def put_r(b, a, v):
            q1[b, pl.ds(BAND + a, 64, stride=2), :] = v

        scatter1(r, put_r)

        def finish(p, c, v):
            m1[p, every2(BAND + c), :] = (other[p, every2(c), :] - v) * times

        soft_rows(q1, 2, 128, 1, finish)

    a2 = ref["a2"]

    def source2_in():
        arrived("s2a", r_s2a)
        for h in range(2):
            a2[h] = r_s2a[:, 128 * h : 128 * h + 128] * LOG2E

    transform1("l1a", b1, source2_in)
    transform1("l1b", a1, lambda: None)
    transform1("l1c", b1, lambda: None, 2.0)

    w2, u2, l2ps, l2pr = ref["w2"], ref["u2"], ref["l2ps"], ref["l2pr"]

    def put_w2(p, c, s, v):
        w2[pl.ds(64 * p + 2 * c + s, 32, stride=2), :] = v

    soft_rows_copied(m1, 2, pl.multiple_of(32 * zh, 32), 32, 2, put_w2)
    u2[0, pl.ds(BAND, 128), :] = w2[...].T
    w3 = ref["w3"]

    def put_w3(p, c, s, v):
        w3[0, pl.ds(2 * c + s, 32, stride=2), :] = v

    soft_rows_copied(u2, 1, 0, 128, 2, put_w3)
    for h in range(2):
        t = w3[0, 128 * h : 128 * h + 128, :].T
        for a in range(2):
            l2ps[h, pl.ds(a, 64, stride=2), :] = t[64 * a : 64 * a + 64]
    exchange(
        "l2p", 64, g, in_group,
        lambda q: l2ps.at[:, pl.ds(2 * (32 * (q % 2) + q // 2), 2)],
        lambda q: l2pr.at[:, pl.ds(BAND + 2 * q, 2)],
        l2pr.at[:, pl.ds(0, 126)],
    )
    arrived("l2p", l2pr.at[:, pl.ds(BAND, 128)])
    m2, k2, fbr = ref["m2"], ref["k2"], ref["fbr"]

    def put_m2(p, c, s, v):
        m2[p, pl.ds(BAND + 2 * c + s, 32, stride=2), :] = a2[p, pl.ds(2 * c + s, 32, stride=2), :] - v

    soft_rows_copied(l2pr, 2, 0, 128, 2, put_m2)
    exchange(
        "fb", 32, px, pencil,
        lambda q: m2.at[:, pl.ds(BAND + 8 * q, 8)],
        lambda q: fbr.at[:, pl.ds(8 * q, 8)],
        fbr.at[:, pl.ds(0, 248)],
    )

    def put_w(p, c, v):
        w3[p, every2(c), :] = v

    def turn2(store):
        for i in range(2):
            for j in range(2):
                store(i, j, w3[j, 128 * i : 128 * i + 128, :].T)

    def put_k2(i, j, v):
        k2[i, pl.ds(BAND + 128 * j, 128), :] = v

    soft_rows(m2, 2, 256, 2, put_w)
    turn2(put_k2)
    l2s, l2r = ref["l2s"], ref["l2r"]

    low = px < 16
    beside = jnp.where(low, py - 1, py + 1)
    has_beside = (beside >= 0) & (beside < 8)
    k_own = ROUNDS.index("l2own")
    k_beside = jnp.where(low, ROUNDS.index("l2down"), ROUNDS.index("l2up"))
    place = jnp.where(low, 48 + px, px - 16)

    def last_send(k, q, row, y):
        pltpu.make_async_remote_copy(
            src_ref=l2s.at[:, pl.ds(8 * q, 8)],
            dst_ref=l2r.at[row],
            send_sem=send_sem.at[k],
            recv_sem=recv_sem.at[k],
            device_id=(q, y),
            device_id_type=MESH,
        ).start()

    def last_own():
        pltpu.make_async_copy(l2s.at[:, pl.ds(8 * px, 8)], l2r.at[BAND + px], recv_sem.at[k_own]).start()

    for i in range(2):

        def put_half(p, c, v, i=i):
            w3[i, every2(c), :] = v

        soft_rows(k2.at[pl.ds(i, 1)], 1, 256, 2, put_half)
        for h in range(2):
            l2s[h, 128 * i : 128 * i + 128, :] = w3[i, 128 * h : 128 * h + 128, :].T
        to = [16 * i + 4 * near[1][dy] + near[0][dx] for dx, dy, dz, dc in FAR_FIRST if dz == dc == 0]
        to = to + [16 * i + px % 16]

        def beside_half(to=to):
            for q in to:
                last_send(k_beside, q, place, beside)

        pl.when(has_beside)(beside_half)
        for q in to[:-1]:
            last_send(k_own, q, BAND + px, py)
        pl.when(px // 16 != i)(functools.partial(last_send, k_own, to[-1], BAND + px, py))
    last_own()
    leaving.append(("l2own", l2r.at[pl.ds(0, 31)]))

    arrived("fb", fbr)
    for d in range(8):
        for h in range(2):
            f_out[d, :, 128 * h : 128 * h + 128] = fbr[h, pl.ds(d, 32, stride=8), :]
    write_f = pltpu.make_async_copy(f_out, f_into, io_sem.at[2])
    write_f.start()

    arrived("l2own", l2r.at[pl.ds(BAND, 32)])
    edge = jnp.full((BAND, 2, 8, 128), NEG, jnp.float32)

    @pl.when(py > 0)
    def _():
        arrived("l2up", l2r.at[pl.ds(0, BAND)])

    @pl.when(py == 0)
    def _():
        l2r[pl.ds(0, BAND)] = edge

    @pl.when(py < 7)
    def _():
        arrived("l2down", l2r.at[pl.ds(48, BAND)])

    @pl.when(py == 7)
    def _():
        l2r[pl.ds(48, BAND)] = edge

    def put_rows(r, h, v):
        w3[h, pl.ds(r, 8, stride=32), :] = v

    soft_major(l2r, 32, 2, put_rows)
    for h in range(2):
        cols = slice(128 * h, 128 * h + 128)
        for d in range(8):
            g_out[d, :, cols] = w3[h, 32 * d : 32 * d + 32, :]
    write_g = pltpu.make_async_copy(g_out, g_into, io_sem.at[3])
    write_g.start()

    @pl.when(has_beside & low)
    def _():
        sent("l2down", l2r.at[pl.ds(0, 32)])

    @pl.when(has_beside & jnp.logical_not(low))
    def _():
        sent("l2up", l2r.at[pl.ds(0, 32)])

    write_f.wait()
    write_g.wait()
    for name, part in leaving:
        sent(name, part)
    sent("x0", x0r.at[pl.ds(0, 62)])
    sent("g0", b0.at[pl.ds(0, 56)])
    pl.when(own // 4 != py)(lambda: sent("x0", x0r.at[pl.ds(0, 2)]))
    pl.when(own != px)(lambda: sent("g0", b0.at[pl.ds(0, 8)]))


SCRATCH = [
    ("src", (8, 32, 256)), ("tgt", (8, 32, 256)), ("f", (8, 32, 256)), ("g", (8, 32, 256)),
    ("g0s", (2, 8, 128)),
    ("g1s", (2, 4, 16, 128)), ("g1r", (8, 2, 2, 16, 128)),
    ("s2ar", (256, 256)),
    ("x0r", (64, 128)),
    ("l0as", (64, 128)), ("l0ar", (64, 128)), ("l0bs", (64, 128)), ("l0br", (64, 128)),
    ("l0cs", (64, 128)), ("l0cr", (64, 128)),
    ("x1s", (2, 128, 128)), ("x1r", (2, 128, 128)),
    ("l1ps", (128, 128)), ("l1pr", (128, 128)),
    ("l1as", (2, 128, 128)), ("l1ar", (2, 128, 128)), ("l1bs", (2, 128, 128)), ("l1br", (2, 128, 128)),
    ("l1cs", (2, 128, 128)), ("l1cr", (2, 128, 128)),
    ("l2ps", (2, 128, 128)), ("l2pr", (2, 160, 128)),
    ("l2s", (2, 256, 128)), ("l2r", (64, 2, 8, 128)),
    ("fbr", (2, 256, 128)),
    ("m0", (1, 96, 128)), ("t0", (1, 96, 128)), ("r0", (1, 96, 128)), ("w0", (64, 128)),
    ("a0", (64, 128)), ("b0", (64, 128)),
    ("m1", (2, 160, 128)), ("t1", (2, 160, 128)), ("r1", (2, 160, 128)), ("w1", (2, 128, 128)),
    ("a1", (2, 128, 128)), ("b1", (2, 128, 128)),
    ("c1", (1, 96, 128)), ("u1", (128, 128)),
    ("u2", (1, 160, 128)), ("w2", (128, 128)), ("a2", (2, 256, 128)),
    ("m2", (2, 288, 128)), ("k2", (2, 288, 128)), ("w3", (2, 256, 128)),
]


def per_device(log_source, log_target):
    shape = jax.ShapeDtypeStruct((8, 32, 256), jnp.float32)
    anywhere = pl.BlockSpec(memory_space=pl.ANY)
    scaled_f, pulled = pl.pallas_call(
        kernel,
        out_shape=(shape, shape),
        in_specs=[anywhere, anywhere],
        out_specs=(anywhere, anywhere),
        scratch_shapes=[pltpu.VMEM(s, jnp.float32) for _, s in SCRATCH]
        + [pltpu.SemaphoreType.DMA((4,)), pltpu.SemaphoreType.DMA((len(ROUNDS),)), pltpu.SemaphoreType.DMA((len(ROUNDS),))],
        compiler_params=pltpu.CompilerParams(collective_id=0, has_side_effects=True),
        name="sinkhorn",
    )(log_source, log_target)
    return 0.05 * LN2 * scaled_f, 0.05 * log_target - 0.05 * LN2 * pulled


def solution(mesh):
    return jax.shard_map(
        per_device,
        mesh=mesh,
        in_specs=(P("px", "py", None), P("px", "py", None)),
        out_specs=(P("px", "py", None), P("px", "py", None)),
        check_vma=False,
    )
```
